128 devices in a mesh: blk: 32 (over x, y, core), head: 4 (over z).
Axes of the slice: x: 4, y: 4, z: 4, core: 2. Of those that a mesh axis runs over, the one named last changes fastest.
Arguments:
- queries: bfloat16 [8192, 512], P(('blk', 'head')), may hold values from -6 to 6
- keys: bfloat16 [8192, 512], P(('blk', 'head')), may hold values from -6 to 6
- values: bfloat16 [8192, 512], P(('blk', 'head')), may hold values from -6 to 6
- out_grad: bfloat16 [8192, 512], P(('blk', 'head')), may hold values from -6 to 6
- tile_mask: int32 [64, 64], replicated, may hold values from 0 to 1, as said below
- frame_order: int32 [32], replicated, may hold values from 0 to 31, each once
Outputs:
- query_grad: bfloat16 [8192, 512], P(('blk', 'head'))
- key_grad: bfloat16 [8192, 512], P(('blk', 'head'))
- value_grad: bfloat16 [8192, 512], P(('blk', 'head'))
The draws below stay inside these ranges and needn't reach their ends.
Inputs may be any that keep to these rules, and one draw needn't show every extreme that they name: `tile_mask`: 1 where a query tile may attend a key tile, else 0; every tile may attend all tiles of its own frame. Shard b of blk holds frame frame_order[b]; each frame once.
All inputs are finite; a program needn't handle non-finite values.
Results may differ from the reference program's by a relative error of at most 0.0024.
The reference program's roundings to bfloat16 on the way (of `probs_half`, `attention_out` and `score_grad`) count: a program that leaves them out, or rounds other values in their place, can miss the bound.
Values may be sent and summed in bfloat16 or wider, within the bound.
A program may use at most 64 MiB of HBM per device.

```python
import jax
import jax.numpy as jnp
from jax import lax

HEADS = 8
HDIM = 64
D = 512
PATCHES = 256
TILE = 128
WINDOW = 16
FRAMES = 32
TOKENS = 8192


def drawn(key, salt_value):
    shape = (FRAMES * PATCHES, HEADS * HDIM)
    field_key = jax.random.fold_in(key, salt_value)
    values_field = jnp.clip(jax.random.normal(field_key, shape, jnp.float32), -6.0, 6.0)
    return values_field


def draw_queries(key, part):
    return drawn(key, 11).astype(jnp.bfloat16)


def draw_keys(key, part):
    return drawn(key, 21).astype(jnp.bfloat16)


def draw_tile_mask(key, part):
    tiles_per = PATCHES // TILE
    tile_count = FRAMES * tiles_per
    tile_index = jnp.arange(tile_count, dtype=jnp.int32)
    frame_index = tile_index // tiles_per
    place_index = tile_index % tiles_per
    frame_gap = frame_index[:, None] - frame_index[None, :]
    adjacent = jnp.abs(place_index[:, None] - place_index[None, :]) <= 1
    random_bits = jax.random.randint(key, (tile_count, tile_count), 0, 2)
    earlier = (frame_gap >= 1) & (frame_gap <= WINDOW) & adjacent
    return jnp.where(frame_gap == 0, 1, jnp.where(earlier, random_bits, 0)).astype(jnp.int32)


def shard_levels(own_key, shape, shards, low, largest):
    factor_of = 1.0
    for position, blocks in shards:
        draws = jax.random.uniform(jax.random.fold_in(jax.random.fold_in(own_key, 6), position), (blocks,), jnp.float32, low / len(shards), largest / len(shards))
        factor_of = factor_of * jnp.repeat(jnp.exp(draws), shape[position] // blocks).reshape((-1,) + (1,) * (len(shape) - 1 - position))
    return factor_of


def noise(own_key, shape, spread, limit, shards=(), kind=jnp.bfloat16):
    array = jax.random.normal(own_key, shape, jnp.float32) * spread
    if len(shards) > 0:
        array = shard_levels(own_key, shape, shards, -0.22, 0.18) * array
    return jnp.clip(array, min=-limit, max=limit).astype(kind)


def setup_inputs(seed: int = 0) -> dict:
    streams_of = jax.random.split(jax.random.key(seed), 7)
    return {
        "queries": draw_queries(jax.random.fold_in(streams_of[6], 71), 0),
        "keys": draw_keys(jax.random.fold_in(streams_of[6], 71), 0),
        "values": noise(streams_of[2], (TOKENS, D), 1.0, 6.0, ((0, 128),)),
        "out_grad": noise(streams_of[3], (TOKENS, D), 1.0, 6.0, ((0, 128),)),
        "tile_mask": draw_tile_mask(jax.random.fold_in(streams_of[6], 71), 0),
        "frame_order": jax.random.permutation(streams_of[5], FRAMES).astype(jnp.int32),
    }


NEGATIVE = -1.0e30


def token_tiles(frame_order):
    places = jnp.arange(FRAMES * PATCHES, dtype=jnp.int32)
    frames = jnp.take(frame_order, places // PATCHES)
    return (frames * (PATCHES // TILE) + (places % PATCHES) // TILE).astype(jnp.int32)


def rounded(matrix):
    return lax.optimization_barrier(matrix.astype(jnp.bfloat16)).astype(jnp.float32)


def reference(queries, keys, values, out_grad, tile_mask, frame_order):
    score_scale = HDIM ** -0.5
    tiles = token_tiles(frame_order)

    def heads_first(matrix):
        return matrix.astype(jnp.float32).reshape(TOKENS, HEADS, HDIM).transpose(1, 0, 2)

    stacked = (heads_first(queries), heads_first(keys), heads_first(values), heads_first(out_grad))
    starts = jnp.arange(FRAMES, dtype=jnp.int32) * PATCHES

    def one_head(arrays):
        query_head, key_head, value_head, grad_head = arrays

        def block_setup(offset):
            query_part = lax.dynamic_slice_in_dim(query_head, offset, PATCHES, 0)
            query_tiles = lax.dynamic_slice_in_dim(tiles, offset, PATCHES, 0)
            allowed = jnp.take(jnp.take(tile_mask, query_tiles, axis=0), tiles, axis=1) == 1
            scores = jnp.dot(query_part, key_head.T, preferred_element_type=jnp.float32) * score_scale
            return query_part, allowed, scores

        def forward(offset):
            query_part, allowed, scores = block_setup(offset)
            row_peak = jnp.max(jnp.where(allowed, scores, NEGATIVE), axis=1)
            row_mass = jnp.sum(jnp.where(allowed, jnp.exp(scores - row_peak[:, None]), 0.0), axis=1)
            log_mass = row_peak + jnp.log(row_mass)
            probs_half = rounded(jnp.where(allowed, jnp.exp(scores - log_mass[:, None]), 0.0))
            attention_out = jnp.dot(probs_half, value_head, preferred_element_type=jnp.float32).astype(jnp.bfloat16)
            return log_mass, attention_out

        log_mass, attention_out = lax.map(forward, starts)
        log_mass = log_mass.reshape(TOKENS)
        attention_out = attention_out.reshape(TOKENS, HDIM)
        row_delta = jnp.sum(grad_head * attention_out.astype(jnp.float32), axis=1)

        def backward(running, offset):
            key_sum, value_sum = running
            query_part, allowed, scores = block_setup(offset)
            mass_part = lax.dynamic_slice_in_dim(log_mass, offset, PATCHES, 0)
            delta_part = lax.dynamic_slice_in_dim(row_delta, offset, PATCHES, 0)
            grad_part = lax.dynamic_slice_in_dim(grad_head, offset, PATCHES, 0)
            probs_full = jnp.where(allowed, jnp.exp(scores - mass_part[:, None]), 0.0)
            probs_half = rounded(probs_full)
            prob_grad = jnp.dot(grad_part, value_head.T, preferred_element_type=jnp.float32)
            score_grad = rounded(probs_full * (prob_grad - delta_part[:, None]))
            query_grad = (jnp.dot(score_grad, key_head, preferred_element_type=jnp.float32) * score_scale).astype(jnp.bfloat16)
            key_sum = key_sum + jnp.dot(score_grad.T, query_part, preferred_element_type=jnp.float32)
            value_sum = value_sum + jnp.dot(probs_half.T, grad_part, preferred_element_type=jnp.float32)
            return (key_sum, value_sum), query_grad

        zeros_head = jnp.zeros((TOKENS, HDIM), jnp.float32)
        (key_sum, value_sum), query_grad = lax.scan(backward, (zeros_head, zeros_head), starts)
        return query_grad.reshape(TOKENS, HDIM), (key_sum * score_scale).astype(jnp.bfloat16), value_sum.astype(jnp.bfloat16)

    query_grad, key_grad, value_grad = lax.map(one_head, stacked)

    def merge_heads(matrix):
        return matrix.transpose(1, 0, 2).reshape(TOKENS, HEADS * HDIM)

    return merge_heads(query_grad), merge_heads(key_grad), merge_heads(value_grad)
```

```python
import functools

import jax
import jax.numpy as jnp
from jax import lax
from jax.experimental import pallas as pl
from jax.experimental.pallas import tpu as pltpu
from jax.sharding import PartitionSpec as P

HDIM = 64
TILE = 128
LANES = 128
HEADS = 8
ROWS = 64
TILES = 4
BLOCK = TILES * TILE
BLOCKS = 16
SLOTS = BLOCKS * TILES
GROUP = 4
PIECES = ((0, 176), (176, 176), (352, 160))
MESH = pl.DeviceIdType.MESH
F32 = jnp.float32
BF16 = jnp.bfloat16
BIG = 1e30
NT = (((1,), (1,)), ((), ()))
NN = (((1,), (0,)), ((), ()))
VMEM_SPEC = pl.BlockSpec(memory_space=pltpu.VMEM)
SMEM_SPEC = pl.BlockSpec(memory_space=pltpu.SMEM)


def here():
    blk = lax.axis_index("blk")
    z = lax.axis_index("head")
    return (blk // 8, (blk // 2) % 4, z), blk % 2


def device(place, core):
    x, y, z = place
    return ((x * 4 + y) * 2 + core, z)


def paired(v, flip):
    return v + (1 - 2 * (v % 2)) if flip else v


def half(v):
    return ((v + 1) // 2) % 2


def head_of(place, offset):
    bits = [(half(v) + d) % 2 for v, d in zip(place, offset)]
    return bits[0] * 4 + bits[1] * 2 + bits[2]


def block_of(place, core, offset=(0, 0, 0)):
    bits = [(v // 2 + d) % 2 for v, d in zip(place, offset)]
    return ((bits[0] * 2 + bits[1]) * 2 + bits[2]) * 2 + core


def entry_rows(place, offset=(0, 0, 0)):
    bits = [(v % 2 + d) % 2 for v, d in zip(place, offset)]
    return pl.multiple_of((bits[0] * 2 + bits[1]) * TILE + bits[2] * ROWS, ROWS)


OFFSETS = [(a, b, c) for a in (0, 1) for b in (0, 1) for c in (0, 1)][1:]


def pair_device(place, core, offset):
    return device([paired(v, d) for v, d in zip(place, offset)], core)


def mirror_device(place, core, axis):
    return device([3 - v if a == axis else v for a, v in enumerate(place)], core)


def remote(src, dst, send, recv, target):
    return pltpu.make_async_remote_copy(
        src_ref=src, dst_ref=dst, send_sem=send, recv_sem=recv, device_id=target, device_id_type=MESH
    )


def greet(targets):
    barrier = pltpu.get_barrier_semaphore()
    for target in targets:
        pl.semaphore_signal(barrier, inc=1, device_id=target, device_id_type=MESH)
    return lambda: pl.semaphore_wait(barrier, len(targets))


UNIT = [(1, 0, 0), (0, 1, 0), (0, 0, 1)]


def plus(*offsets):
    return tuple(sum(v) for v in zip(*offsets))


class CubeGather:
    def __init__(self, ref, place, core, send, recv, core_send, core_recv):
        self.ref, self.place, self.core = ref, place, core
        self.send, self.recv, self.core_send, self.core_recv = send, recv, core_send, core_recv

    def part(self, piece, offset, core=None):
        first, count = PIECES[piece]
        core = self.core if core is None else core
        return self.ref.at[block_of(self.place, core, offset), pl.ds(first, count), :]

    def hops(self, piece):
        a1, a2, a3 = [(piece + i) % 3 for i in range(3)]
        u1, u2, o = UNIT[a1], UNIT[a2], (0, 0, 0)
        return [(a1, o), (a2, o), (a2, u1), (a3, o), (a3, u1), (a3, u2), (a3, plus(u1, u2))]

    def out_copy(self, piece, k):
        axis, offset = self.hops(piece)[k]
        part = self.part(piece, offset)
        return remote(part, part, self.send.at[piece, k], self.recv.at[piece, k],
                      mirror_device(self.place, self.core, axis))

    def in_copy(self, piece, k):
        axis, offset = self.hops(piece)[k]
        part = self.part(piece, plus(offset, UNIT[axis]))
        return remote(part, part, self.send.at[piece, k], self.recv.at[piece, k],
                      mirror_device(self.place, self.core, axis))

    def core_copy(self, piece, k, core=None):
        if k == 7:
            offset = (0, 0, 0)
        else:
            axis, offset = self.hops(piece)[k]
            offset = plus(offset, UNIT[axis])
        part = self.part(piece, offset, core)
        return remote(part, part, self.core_send.at[piece, k], self.core_recv.at[piece, k],
                      device(self.place, 1 - self.core))

    def begin(self):
        for k in (0, 1, 3):
            for p in range(3):
                self.out_copy(p, k).start()
        for p in range(3):
            self.core_copy(p, 7).start()

    def relay(self):
        for k, onward in ((0, (2, 4)), (1, (5,)), (2, (6,)), (3, ()), (4, ()), (5, ()), (6, ())):
            for p in range(3):
                self.in_copy(p, k).wait_recv()
                for j in onward:
                    self.out_copy(p, j).start()
                self.core_copy(p, k).start()

    def finish(self):
        for k in (7, 0, 1, 2, 3, 4, 5, 6):
            for p in range(3):
                self.core_copy(p, k, 1 - self.core).wait_recv()
        for p in range(3):
            for k in range(7):
                self.out_copy(p, k).wait_send()
            for k in range(8):
                self.core_copy(p, k).wait_send()


GATHER_SEMS = [
    pltpu.SemaphoreType.DMA((3, 7)),
    pltpu.SemaphoreType.DMA((3, 7)),
    pltpu.SemaphoreType.DMA((3, 8)),
    pltpu.SemaphoreType.DMA((3, 8)),
]


def low_lanes(rows):
    return lax.broadcasted_iota(jnp.int32, (rows, LANES), 1) < HDIM


def pack_heads(first_ref, second_ref, packed, scale=None):
    low = low_lanes(ROWS)
    for j in range(HEADS // 2):
        columns = slice(j * LANES, (j + 1) * LANES)
        one = first_ref[:, columns].astype(F32)
        two = second_ref[:, columns].astype(F32)
        if scale is not None:
            one = one * scale
        packed[2 * j] = jnp.where(low, one, pltpu.roll(two, HDIM, 1)).astype(BF16)
        packed[2 * j + 1] = jnp.where(low, pltpu.roll(one, HDIM, 1), two).astype(BF16)


def enter_kernel(q_ref, k_ref, v_ref, g_ref, kv_ref, kv_own, qg_own, kv_pack, qg_pack,
                 pair_send, pair_recv, send, recv, core_send, core_recv):
    place, core = here()
    wait_all = greet(
        [pair_device(place, core, o) for o in OFFSETS]
        + [mirror_device(place, core, a) for a in range(3)]
        + [device(place, 1 - core)]
    )
    own = block_of(place, core)
    mine = entry_rows(place)

    def pair_copy(which, i):
        packed = (kv_pack, qg_pack)[which]
        landing = kv_ref.at[own, pl.ds(mine, ROWS), :] if which == 0 else qg_own.at[pl.ds(mine, ROWS), :]
        return remote(packed.at[head_of(place, OFFSETS[i])], landing, pair_send.at[which, i],
                      pair_recv.at[which, i], pair_device(place, core, OFFSETS[i]))

    def pair_arrival(which, i):
        rows = entry_rows(place, OFFSETS[i])
        landing = kv_ref.at[own, pl.ds(rows, ROWS), :] if which == 0 else qg_own.at[pl.ds(rows, ROWS), :]
        packed = (kv_pack, qg_pack)[which]
        return remote(packed.at[head_of(place, OFFSETS[i])], landing, pair_send.at[which, i],
                      pair_recv.at[which, i], pair_device(place, core, OFFSETS[i]))

    pack_heads(k_ref, v_ref, kv_pack)
    wait_all()
    for i in range(7):
        pair_copy(0, i).start()
    kv_ref[own, pl.ds(mine, ROWS), :] = kv_pack[head_of(place, (0, 0, 0))]
    pack_heads(q_ref, g_ref, qg_pack, HDIM ** -0.5)
    for i in range(7):
        pair_copy(1, i).start()
    qg_own[pl.ds(mine, ROWS), :] = qg_pack[head_of(place, (0, 0, 0))]
    for i in range(7):
        pair_arrival(0, i).wait_recv()
    gather = CubeGather(kv_ref, place, core, send, recv, core_send, core_recv)
    gather.begin()
    kv_own[...] = kv_ref[own]
    gather.relay()
    for i in range(7):
        pair_arrival(1, i).wait_recv()
    for which in range(2):
        for i in range(7):
            pair_copy(which, i).wait_send()
    gather.finish()


def enter(q, k, v, g):
    return pl.pallas_call(
        enter_kernel,
        name="enter",
        out_shape=(
            jax.ShapeDtypeStruct((BLOCKS, BLOCK, LANES), BF16),
            jax.ShapeDtypeStruct((BLOCK, LANES), BF16),
            jax.ShapeDtypeStruct((BLOCK, LANES), BF16),
        ),
        in_specs=[VMEM_SPEC] * 4,
        out_specs=(VMEM_SPEC,) * 3,
        scratch_shapes=[
            pltpu.VMEM((HEADS, ROWS, LANES), BF16),
            pltpu.VMEM((HEADS, ROWS, LANES), BF16),
            pltpu.SemaphoreType.DMA((2, 7)),
            pltpu.SemaphoreType.DMA((2, 7)),
        ] + GATHER_SEMS,
        compiler_params=pltpu.CompilerParams(
            collective_id=0, has_side_effects=True, vmem_limit_bytes=16 * 2**20
        ),
    )(q, k, v, g)


def share_kernel(qg_own, stat_own, qg_ref, stat_ref, stat_send, stat_recv, send, recv, core_send, core_recv):
    place, core = here()
    peers = [(o, c) for o in [(0, 0, 0)] + OFFSETS for c in (0, 1)][1:]

    def peer_device(offset, flip):
        mirrored = [3 - v if d else v for v, d in zip(place, offset)]
        return device(mirrored, (core + flip) % 2)

    wait_all = greet([peer_device(*p) for p in peers])
    own = block_of(place, core)
    qg_ref[own] = qg_own[...]
    stat_ref[own] = stat_own[...]
    wait_all()
    gather = CubeGather(qg_ref, place, core, send, recv, core_send, core_recv)

    def stat_copy(i):
        part = stat_ref.at[own]
        return remote(part, part, stat_send.at[i], stat_recv.at[i], peer_device(*peers[i]))

    def stat_arrival(i):
        offset, flip = peers[i]
        part = stat_ref.at[block_of(place, (core + flip) % 2, offset)]
        return remote(part, part, stat_send.at[i], stat_recv.at[i], peer_device(*peers[i]))

    gather.begin()
    for i in range(15):
        stat_copy(i).start()
    gather.relay()
    for i in range(15):
        stat_arrival(i).wait_recv()
    for i in range(15):
        stat_copy(i).wait_send()
    gather.finish()


def share(qg_own, stat_own):
    return pl.pallas_call(
        share_kernel,
        name="share",
        out_shape=(
            jax.ShapeDtypeStruct((BLOCKS, BLOCK, LANES), BF16),
            jax.ShapeDtypeStruct((BLOCKS, 8, LANES), F32),
        ),
        in_specs=[VMEM_SPEC] * 2,
        out_specs=(VMEM_SPEC,) * 2,
        scratch_shapes=[pltpu.SemaphoreType.DMA((15,)), pltpu.SemaphoreType.DMA((15,))] + GATHER_SEMS,
        compiler_params=pltpu.CompilerParams(
            collective_id=1, has_side_effects=True, vmem_limit_bytes=16 * 2**20
        ),
    )(qg_own, stat_own)


def fill_table(order_ref, table):
    for slot in range(SLOTS):
        b, t = slot // TILES, slot % TILES
        x = 2 * (b // 8) + t // 2
        y = 2 * ((b // 4) % 2) + t % 2
        table[slot] = order_ref[(x * 4 + y) * 2 + b % 2] * 2 + (b // 2) % 2


def fill_list(allowed, listed):
    count = jnp.int32(0)
    for slot in range(SLOTS):
        listed[count] = slot
        count = count + allowed(slot)
    first = listed[0]
    for i in range(GROUP - 1):
        listed[count + i] = first
    return count


def query_kernel(kv_ref, qg_own, mask_ref, order_ref, stat_ref, dq_ref, table, listed, score_buf, stat_buf):
    place, core = here()
    own = block_of(place, core)
    fill_table(order_ref, table)
    low = low_lanes(TILE)
    lane = lax.broadcasted_iota(jnp.int32, (TILE, LANES), 1)
    zero = jnp.zeros((TILE, LANES), BF16)
    zeros = jnp.zeros((TILE, LANES), F32)

    def one_tile(t, unused):
        tile = table[own * TILES + t]
        count = fill_list(lambda s: (mask_ref[tile, table[s]] == 1).astype(jnp.int32), listed)
        steps = (count + GROUP - 1) // GROUP
        both = qg_own[t]
        query = jnp.where(low, both, zero)
        grad = jnp.where(low, zero, both)

        def keys_of(step):
            return jnp.concatenate([kv_ref[listed[step * GROUP + u]] for u in range(GROUP)], axis=0)

        def cut(wide, u):
            return wide[:, u * TILE : (u + 1) * TILE]

        def scores_step(step, peak):
            scores = lax.dot_general(query, keys_of(step), NT, preferred_element_type=F32)
            score_buf[step] = scores
            for u in range(GROUP):
                peak = jnp.maximum(peak, cut(scores, u))
            return peak

        peak = lax.fori_loop(0, steps, scores_step, jnp.full((TILE, LANES), -BIG, F32))
        peak = jnp.max(peak, axis=1, keepdims=True)

        def exp_step(step, mass):
            for u in range(GROUP):
                less = jnp.where(step * GROUP + u < count, 0.0, BIG).astype(F32)
                columns = slice(u * TILE, (u + 1) * TILE)
                term = jnp.exp(score_buf[step, :, columns] - (peak + less))
                score_buf[step, :, columns] = term
                mass = mass + term
            return mass

        mass = lax.fori_loop(0, steps, exp_step, zeros)
        mass = jnp.sum(mass, axis=1, keepdims=True)
        inverse = 1.0 / mass
        log_mass = peak + jnp.log(mass)

        def out_step(step, out):
            probs = (score_buf[step] * inverse).astype(BF16)
            return out + lax.dot_general(probs, keys_of(step), NN, preferred_element_type=F32)

        out = lax.fori_loop(0, steps, out_step, zeros)
        out = out.astype(BF16).astype(F32)
        delta = jnp.sum(jnp.where(low, 0.0, both.astype(F32) * out), axis=1, keepdims=True)

        def grad_step(step, acc):
            keys = keys_of(step)
            prob_grad = lax.dot_general(grad, keys, NT, preferred_element_type=F32)
            score_grad = ((score_buf[step] * inverse) * (prob_grad - delta)).astype(BF16)
            return acc + lax.dot_general(score_grad, keys, NN, preferred_element_type=F32)

        acc = lax.fori_loop(0, steps, grad_step, zeros) * HDIM ** -0.5
        low_part = low_lanes(ROWS // 2)
        for i in range(2):
            top = acc[i * ROWS : i * ROWS + ROWS // 2]
            bottom = acc[i * ROWS + ROWS // 2 : (i + 1) * ROWS]
            dq_ref[2 * t + i] = jnp.where(low_part, top, pltpu.roll(bottom, HDIM, 1)).astype(BF16)
        stats = jnp.where(lane == t, log_mass, stat_buf[...])
        stat_buf[...] = jnp.where(lane == TILES + t, delta, stats)
        return unused

    stat_buf[...] = zeros
    lax.fori_loop(0, TILES, one_tile, 0)
    stat_ref[...] = stat_buf[...].T[:8]


def query_side(kv, qg_own, tile_mask, frame_order):
    return pl.pallas_call(
        query_kernel,
        name="query_side",
        out_shape=(
            jax.ShapeDtypeStruct((8, LANES), F32),
            jax.ShapeDtypeStruct((2 * TILES, ROWS // 2, LANES), BF16),
        ),
        in_specs=[VMEM_SPEC, VMEM_SPEC, SMEM_SPEC, SMEM_SPEC],
        out_specs=(VMEM_SPEC,) * 2,
        scratch_shapes=[
            pltpu.SMEM((SLOTS,), jnp.int32),
            pltpu.SMEM((SLOTS + GROUP,), jnp.int32),
            pltpu.VMEM((SLOTS // GROUP, TILE, GROUP * TILE), F32),
            pltpu.VMEM((TILE, LANES), F32),
        ],
        compiler_params=pltpu.CompilerParams(vmem_limit_bytes=24 * 2**20),
    )(kv.reshape(SLOTS, TILE, LANES), qg_own.reshape(TILES, TILE, LANES), tile_mask, frame_order)


def key_kernel(qg_ref, stat_ref, kv_own, mask_ref, order_ref, dkv_ref, table, listed, rows_ref):
    place, core = here()
    own = block_of(place, core)
    fill_table(order_ref, table)
    for b in range(BLOCKS):
        for t in range(TILES):
            rows_ref[b * TILES + t, 0:1, :] = stat_ref[b, t : t + 1, :]
            rows_ref[b * TILES + t, 1:2, :] = stat_ref[b, TILES + t : TILES + t + 1, :]
    low = low_lanes(TILE)
    zero = jnp.zeros((TILE, LANES), BF16)

    def one_tile(t, unused):
        tile = table[own * TILES + t]
        count = fill_list(lambda s: (mask_ref[table[s], tile] == 1).astype(jnp.int32), listed)
        steps = (count + GROUP - 1) // GROUP
        both = kv_own[t]
        stacked = jnp.concatenate([jnp.where(low, both, zero), jnp.where(low, zero, both)], axis=0)

        def step_terms(step, acc):
            lefts, rights = [], []
            for u in range(GROUP):
                slot = listed[step * GROUP + u]
                less = jnp.where(step * GROUP + u < count, 0.0, BIG).astype(F32)
                queries = qg_ref[slot]
                products = lax.dot_general(stacked, queries, NT, preferred_element_type=F32)
                probs = jnp.exp(products[:TILE] - (rows_ref[slot, 0:1, :] + less))
                score_grad = probs * (products[TILE:] - rows_ref[slot, 1:2, :])
                lefts += [score_grad.astype(BF16), probs.astype(BF16)]
                rights += [jnp.where(low, queries, zero), jnp.where(low, zero, queries)]
            return acc + lax.dot_general(
                jnp.concatenate(lefts, axis=1), jnp.concatenate(rights, axis=0), NN,
                preferred_element_type=F32,
            )

        acc = lax.fori_loop(0, steps, step_terms, jnp.zeros((TILE, LANES), F32))
        dkv_ref[t] = acc.astype(BF16)
        return unused

    lax.fori_loop(0, TILES, one_tile, 0)


def key_side(qg, stats, kv_own, tile_mask, frame_order):
    return pl.pallas_call(
        key_kernel,
        name="key_side",
        out_shape=jax.ShapeDtypeStruct((TILES, TILE, LANES), BF16),
        in_specs=[VMEM_SPEC, VMEM_SPEC, VMEM_SPEC, SMEM_SPEC, SMEM_SPEC],
        out_specs=VMEM_SPEC,
        scratch_shapes=[
            pltpu.SMEM((SLOTS,), jnp.int32),
            pltpu.SMEM((SLOTS + GROUP,), jnp.int32),
            pltpu.VMEM((SLOTS, 8, LANES), F32),
        ],
        compiler_params=pltpu.CompilerParams(vmem_limit_bytes=24 * 2**20),
    )(qg.reshape(SLOTS, TILE, LANES), stats, kv_own.reshape(TILES, TILE, LANES), tile_mask, frame_order)


def leave_kernel(dq_ref, dkv_ref, q_out, k_out, v_out, dq_got, dkv_got, pair_send, pair_recv):
    place, core = here()
    wait_all = greet([pair_device(place, core, o) for o in OFFSETS])
    mine = head_of(place, (0, 0, 0))
    sources, landings = (dq_ref, dkv_ref), (dq_got, dkv_got)

    def share_of(offset):
        bits = [(v % 2 + d) % 2 for v, d in zip(place, offset)]
        return (bits[0] * 2 + bits[1]) * 2 + bits[2]

    def pair_copy(which, i):
        return remote(sources[which].at[share_of(OFFSETS[i])], landings[which].at[mine],
                      pair_send.at[which, i], pair_recv.at[which, i], pair_device(place, core, OFFSETS[i]))

    def pair_arrival(which, i):
        return remote(sources[which].at[share_of(OFFSETS[i])], landings[which].at[head_of(place, OFFSETS[i])],
                      pair_send.at[which, i], pair_recv.at[which, i], pair_device(place, core, OFFSETS[i]))

    wait_all()
    for which in (1, 0):
        for i in range(7):
            pair_copy(which, i).start()
    dq_got[mine] = dq_ref[share_of((0, 0, 0))]
    dkv_got[mine] = dkv_ref[share_of((0, 0, 0))]
    for i in range(7):
        pair_arrival(1, i).wait_recv()
    low = low_lanes(ROWS)
    for j in range(HEADS // 2):
        columns = slice(j * LANES, (j + 1) * LANES)
        one = dkv_got[2 * j].astype(F32)
        two = dkv_got[2 * j + 1].astype(F32)
        k_out[:, columns] = jnp.where(low, one, pltpu.roll(two, HDIM, 1)).astype(BF16)
        v_out[:, columns] = jnp.where(low, pltpu.roll(one, HDIM, 1), two).astype(BF16)
    for i in range(7):
        pair_arrival(0, i).wait_recv()
    low = low_lanes(ROWS // 2)
    for j in range(HEADS // 2):
        columns = slice(j * LANES, (j + 1) * LANES)
        one = dq_got[2 * j].astype(F32)
        two = dq_got[2 * j + 1].astype(F32)
        q_out[0 : ROWS // 2, columns] = jnp.where(low, one, pltpu.roll(two, HDIM, 1)).astype(BF16)
        q_out[ROWS // 2 : ROWS, columns] = jnp.where(low, pltpu.roll(one, HDIM, 1), two).astype(BF16)
    for which in (1, 0):
        for i in range(7):
            pair_copy(which, i).wait_send()


def leave(dq, dkv):
    return pl.pallas_call(
        leave_kernel,
        name="leave",
        out_shape=(jax.ShapeDtypeStruct((ROWS, HEADS * HDIM), BF16),) * 3,
        in_specs=[VMEM_SPEC] * 2,
        out_specs=(VMEM_SPEC,) * 3,
        scratch_shapes=[
            pltpu.VMEM((HEADS, ROWS // 2, LANES), BF16),
            pltpu.VMEM((HEADS, ROWS, LANES), BF16),
            pltpu.SemaphoreType.DMA((2, 7)),
            pltpu.SemaphoreType.DMA((2, 7)),
        ],
        compiler_params=pltpu.CompilerParams(
            collective_id=2, has_side_effects=True, vmem_limit_bytes=8 * 2**20
        ),
    )(dq, dkv.reshape(HEADS, ROWS, LANES))


def body(queries, keys, values, out_grad, tile_mask, frame_order):
    kv, kv_own, qg_own = enter(queries, keys, values, out_grad)
    stats_own, dq = query_side(kv, qg_own, tile_mask, frame_order)
    qg, stats = share(qg_own, stats_own)
    dkv = key_side(qg, stats, kv_own, tile_mask, frame_order)
    return leave(dq, dkv)


def solution(mesh):
    whole = P(("blk", "head"), None)
    return jax.shard_map(
        body,
        mesh=mesh,
        in_specs=(whole,) * 4 + (P(), P()),
        out_specs=(whole,) * 3,
        check_vma=False,
    )
```

```python
import functools

import jax
import jax.numpy as jnp
from jax import lax
from jax.experimental import pallas as pl
from jax.experimental.pallas import tpu as pltpu
from jax.sharding import PartitionSpec as P

HDIM = 64
TILE = 128
LANES = 128
HEADS = 8
ROWS = 64
TILES = 4
BLOCK = TILES * TILE
BLOCKS = 16
SLOTS = BLOCKS * TILES
GROUP = 8
PIECES = ((0, 176), (176, 176), (352, 160))
MESH = pl.DeviceIdType.MESH
F32 = jnp.float32
BF16 = jnp.bfloat16
BIG = 1e30
NT = (((1,), (1,)), ((), ()))
NN = (((1,), (0,)), ((), ()))
HBM_SPEC = pl.BlockSpec(memory_space=pltpu.HBM)
VMEM_SPEC = pl.BlockSpec(memory_space=pltpu.VMEM)
SMEM_SPEC = pl.BlockSpec(memory_space=pltpu.SMEM)


def here():
    blk = lax.axis_index("blk")
    z = lax.axis_index("head")
    return (blk // 8, (blk // 2) % 4, z), blk % 2


def device(place, core):
    x, y, z = place
    return ((x * 4 + y) * 2 + core, z)


def paired(v, flip):
    return v + (1 - 2 * (v % 2)) if flip else v


def half(v):
    return ((v + 1) // 2) % 2


def head_of(place, offset):
    bits = [(half(v) + d) % 2 for v, d in zip(place, offset)]
    return bits[0] * 4 + bits[1] * 2 + bits[2]


def block_of(place, core, offset=(0, 0, 0)):
    bits = [(v // 2 + d) % 2 for v, d in zip(place, offset)]
    return ((bits[0] * 2 + bits[1]) * 2 + bits[2]) * 2 + core


def entry_rows(place, offset=(0, 0, 0)):
    bits = [(v % 2 + d) % 2 for v, d in zip(place, offset)]
    return pl.multiple_of((bits[0] * 2 + bits[1]) * TILE + bits[2] * ROWS, ROWS)


ALL_OFFSETS = [(a, b, c) for a in (0, 1) for b in (0, 1) for c in (0, 1)]
OFFSETS = ALL_OFFSETS[1:]


def pair_device(place, core, offset):
    return device([paired(v, d) for v, d in zip(place, offset)], core)


def mirror_device(place, core, axis):
    return device([3 - v if a == axis else v for a, v in enumerate(place)], core)


def remote(src, dst, send, recv, target):
    return pltpu.make_async_remote_copy(
        src_ref=src, dst_ref=dst, send_sem=send, recv_sem=recv, device_id=target, device_id_type=MESH
    )


def greet(targets):
    barrier = pltpu.get_barrier_semaphore()
    for target in targets:
        pl.semaphore_signal(barrier, inc=1, device_id=target, device_id_type=MESH)
    return lambda: pl.semaphore_wait(barrier, len(targets))


UNIT = [(1, 0, 0), (0, 1, 0), (0, 0, 1)]


def plus(*offsets):
    return tuple(sum(v) for v in zip(*offsets))


class CubeGather:
    def __init__(self, ref, place, core, sems):
        self.ref, self.place, self.core = ref, place, core
        self.send, self.recv, self.core_send, self.core_recv = sems
        self.pieces = [0] * len(ALL_OFFSETS)

    def hops(self, piece):
        a1, a2, a3 = [(piece + i) % 3 for i in range(3)]
        u1, u2, o = UNIT[a1], UNIT[a2], (0, 0, 0)
        return [(a1, o), (a2, o), (a2, u1), (a3, o), (a3, u1), (a3, u2), (a3, plus(u1, u2))]

    def hop_copy(self, piece, k, arriving=False):
        axis, offset = self.hops(piece)[k]
        if arriving:
            offset = plus(offset, UNIT[axis])
        first, count = PIECES[piece]
        part = self.ref.at[block_of(self.place, self.core, offset), pl.ds(first, count), :]
        return remote(part, part, self.send.at[piece, k], self.recv.at[piece, k],
                      mirror_device(self.place, self.core, axis))

    def core_copy(self, i, arriving=False):
        core = 1 - self.core if arriving else self.core
        part = self.ref.at[block_of(self.place, core, ALL_OFFSETS[i])]
        return remote(part, part, self.core_send.at[i], self.core_recv.at[i],
                      device(self.place, 1 - self.core))

    def begin(self):
        for k in (0, 1, 3):
            for p in range(3):
                self.hop_copy(p, k).start()
        self.core_copy(0).start()

    def relay_step(self, k, onward):
        for p in range(3):
            self.hop_copy(p, k, True).wait_recv()
            for j in onward:
                self.hop_copy(p, j).start()
            axis, offset = self.hops(p)[k]
            i = ALL_OFFSETS.index(plus(offset, UNIT[axis]))
            self.pieces[i] += 1
            if self.pieces[i] == 3:
                self.core_copy(i).start()

    def finish(self):
        for i in range(8):
            self.core_copy(i, True).wait_recv()
        for p in range(3):
            for k in range(7):
                self.hop_copy(p, k).wait_send()
        for i in range(8):
            self.core_copy(i).wait_send()


GATHER_SEMS = [
    pltpu.SemaphoreType.DMA((3, 7)),
    pltpu.SemaphoreType.DMA((3, 7)),
    pltpu.SemaphoreType.DMA((8,)),
    pltpu.SemaphoreType.DMA((8,)),
]


def low_lanes(rows):
    return lax.broadcasted_iota(jnp.int32, (rows, LANES), 1) < HDIM


def pack_heads(first_ref, second_ref, packed, scale=None):
    low = low_lanes(ROWS)
    for j in range(HEADS // 2):
        columns = slice(j * LANES, (j + 1) * LANES)
        one = first_ref[:, columns].astype(F32)
        two = second_ref[:, columns].astype(F32)
        if scale is not None:
            one = one * scale
        packed[2 * j] = jnp.where(low, one, pltpu.roll(two, HDIM, 1)).astype(BF16)
        packed[2 * j + 1] = jnp.where(low, pltpu.roll(one, HDIM, 1), two).astype(BF16)


def slot_lists(mask, order, place, core):
    def dot(a, b, dims=NN):
        return lax.dot_general(a.astype(BF16), b.astype(BF16), dims, preferred_element_type=F32)

    def iota(shape, dim):
        return lax.broadcasted_iota(jnp.int32, shape, dim)

    def one_if(condition):
        return jnp.where(condition, 1.0, 0.0).astype(F32)

    slot = iota((32, SLOTS), 1)
    x = 2 * (slot >> 5) + ((slot >> 1) & 1)
    y = 2 * ((slot >> 4) & 1) + (slot & 1)
    from_frame = one_if((x * 4 + y) * 2 + ((slot >> 2) & 1) == iota((32, SLOTS), 0))
    frames = dot(jnp.broadcast_to(order.astype(F32), (8, 32)), from_frame)
    tiles = (2.0 * frames + ((iota((8, SLOTS), 1) >> 3) & 1).astype(F32))[0:1]
    is_tile = one_if(iota((SLOTS, SLOTS), 0).astype(F32) == tiles)
    row = iota((8, SLOTS), 0)
    is_own = one_if(iota((8, SLOTS), 1) == block_of(place, core) * TILES + (row & 3))
    own_tiles = dot(is_own, is_tile, NT)
    mask = one_if(mask == 1)
    attends = dot(dot(own_tiles, mask), is_tile)
    attended = dot(dot(own_tiles, mask, NT), is_tile)
    allowed = jnp.where(row < TILES, attends, attended)
    ahead = dot(allowed, one_if(iota((SLOTS, SLOTS), 0) < iota((SLOTS, SLOTS), 1)))
    count = jnp.sum(allowed, axis=1, keepdims=True)
    ahead = jnp.where(allowed > 0.5, ahead, -1.0)
    place_in_list = iota((LANES, SLOTS), 0).astype(F32)
    slots = iota((8, SLOTS), 1).astype(F32)
    lists = jnp.zeros((8, LANES), F32)
    rows, lanes = iota((8, LANES), 0), iota((8, LANES), 1)
    for r in range(8):
        lists = jnp.where(rows == r, dot(slots, one_if(place_in_list == ahead[r : r + 1]), NT), lists)
    lists = jnp.where(lanes.astype(F32) < count, lists, lists[:, 0:1])
    return jnp.where(lanes == LANES - 1, count, lists).astype(jnp.int32)


def enter_kernel(q_ref, k_ref, v_ref, g_ref, mask_ref, order_ref, kv_ref, qg_ref, kv_own, qg_own, list_ref,
                 q_buf, k_buf, v_buf, g_buf, mask_buf, order_buf, kv_pack, qg_pack, load_sems,
                 pair_send, pair_recv, *gather_sems):
    place, core = here()
    wait_all = greet(
        [pair_device(place, core, o) for o in OFFSETS]
        + [mirror_device(place, core, a) for a in range(3)]
        + [device(place, 1 - core)]
    )
    loads = [
        pltpu.make_async_copy(source, target, load_sems.at[i])
        for i, (source, target) in enumerate([
            (k_ref, k_buf), (v_ref, v_buf), (q_ref, q_buf), (g_ref, g_buf),
            (mask_ref, mask_buf), (order_ref, order_buf),
        ])
    ]
    for load in loads:
        load.start()
    own = block_of(place, core)
    packs, whole = (kv_pack, qg_pack), (kv_ref, qg_ref)

    def pair_copy(which, i, arriving=False):
        rows = entry_rows(place, OFFSETS[i] if arriving else (0, 0, 0))
        return remote(packs[which].at[head_of(place, OFFSETS[i])], whole[which].at[own, pl.ds(rows, ROWS), :],
                      pair_send.at[which, i], pair_recv.at[which, i], pair_device(place, core, OFFSETS[i]))

    def hand_out(which):
        for i in range(7):
            pair_copy(which, i).start()
        here_too = packs[which][head_of(place, (0, 0, 0))]
        whole[which][own, pl.ds(entry_rows(place), ROWS), :] = here_too

    gathers = [CubeGather(whole[i], place, core, gather_sems[4 * i : 4 * i + 4]) for i in range(2)]
    loads[0].wait()
    loads[1].wait()
    pack_heads(k_buf, v_buf, kv_pack)
    wait_all()
    hand_out(0)
    loads[2].wait()
    loads[3].wait()
    pack_heads(q_buf, g_buf, qg_pack, HDIM ** -0.5)
    hand_out(1)
    loads[4].wait()
    loads[5].wait()
    list_ref[...] = slot_lists(mask_buf[...], order_buf[...], place, core)
    for which in range(2):
        for i in range(7):
            pair_copy(which, i, True).wait_recv()
        gathers[which].begin()
        (kv_own, qg_own)[which][...] = whole[which][own]
    for k, onward in ((0, (2, 4)), (1, (5,)), (2, (6,)), (3, ()), (4, ()), (5, ()), (6, ())):
        for gather in gathers:
            gather.relay_step(k, onward)
    for which in range(2):
        for i in range(7):
            pair_copy(which, i).wait_send()
    for gather in gathers:
        gather.finish()


def enter(q, k, v, g, tile_mask, frame_order):
    entry = pltpu.VMEM((ROWS, HEADS * HDIM), BF16)
    pack = pltpu.VMEM((HEADS, ROWS, LANES), BF16)
    return pl.pallas_call(
        enter_kernel,
        name="enter",
        out_shape=(
            jax.ShapeDtypeStruct((BLOCKS, BLOCK, LANES), BF16),
            jax.ShapeDtypeStruct((BLOCKS, BLOCK, LANES), BF16),
            jax.ShapeDtypeStruct((BLOCK, LANES), BF16),
            jax.ShapeDtypeStruct((BLOCK, LANES), BF16),
            jax.ShapeDtypeStruct((8, LANES), jnp.int32),
        ),
        in_specs=[HBM_SPEC] * 6,
        out_specs=(VMEM_SPEC,) * 5,
        scratch_shapes=[entry] * 4 + [
            pltpu.VMEM(tile_mask.shape, jnp.int32),
            pltpu.VMEM((1, frame_order.shape[0]), jnp.int32),
            pack,
            pack,
            pltpu.SemaphoreType.DMA((6,)),
            pltpu.SemaphoreType.DMA((2, 7)),
            pltpu.SemaphoreType.DMA((2, 7)),
        ] + GATHER_SEMS * 2,
        compiler_params=pltpu.CompilerParams(
            collective_id=0, has_side_effects=True, vmem_limit_bytes=16 * 2**20
        ),
    )(*[pltpu.with_memory_space_constraint(a, pltpu.HBM) for a in (q, k, v, g, tile_mask, frame_order.reshape(1, -1))])


def share_kernel(stat_own, stat_ref, send, recv):
    place, core = here()
    peers = [(o, c) for o in ALL_OFFSETS for c in (0, 1)][1:]

    def peer_device(offset, flip):
        mirrored = [3 - v if d else v for v, d in zip(place, offset)]
        return device(mirrored, (core + flip) % 2)

    wait_all = greet([peer_device(*p) for p in peers])
    own = block_of(place, core)
    stat_ref[own] = stat_own[...]

    def stat_copy(i, arriving=False):
        offset, flip = peers[i]
        source = block_of(place, (core + flip) % 2, offset) if arriving else own
        part = stat_ref.at[source]
        return remote(part, part, send.at[i], recv.at[i], peer_device(offset, flip))

    wait_all()
    for i in range(15):
        stat_copy(i).start()
    for i in range(15):
        stat_copy(i, True).wait_recv()
    for i in range(15):
        stat_copy(i).wait_send()


def share(stat_own):
    return pl.pallas_call(
        share_kernel,
        name="share",
        out_shape=jax.ShapeDtypeStruct((BLOCKS, 8, LANES), F32),
        in_specs=[VMEM_SPEC],
        out_specs=VMEM_SPEC,
        scratch_shapes=[pltpu.SemaphoreType.DMA((15,)), pltpu.SemaphoreType.DMA((15,))],
        compiler_params=pltpu.CompilerParams(
            collective_id=1, has_side_effects=True, vmem_limit_bytes=4 * 2**20
        ),
    )(stat_own)


def query_kernel(kv_ref, qg_own, list_ref, stat_ref, dq_ref, score_buf, stat_buf):
    low = low_lanes(TILE)
    lane = lax.broadcasted_iota(jnp.int32, (TILE, LANES), 1)
    zero = jnp.zeros((TILE, LANES), BF16)
    zeros = jnp.zeros((TILE, LANES), F32)

    def one_tile(t, unused):
        count = list_ref[t, LANES - 1]
        steps = (count + GROUP - 1) // GROUP
        both = qg_own[t]
        query = jnp.where(low, both, zero)
        grad = jnp.where(low, zero, both)

        def keys_of(step):
            return jnp.concatenate([kv_ref[list_ref[t, step * GROUP + u]] for u in range(GROUP)], axis=0)

        def cut(wide, u):
            return wide[:, u * TILE : (u + 1) * TILE]

        def scores_step(step, peak):
            scores = lax.dot_general(query, keys_of(step), NT, preferred_element_type=F32)
            score_buf[step] = scores
            for u in range(GROUP):
                peak = jnp.maximum(peak, cut(scores, u))
            return peak

        peak = lax.fori_loop(0, steps, scores_step, jnp.full((TILE, LANES), -BIG, F32))
        peak = jnp.max(peak, axis=1, keepdims=True)

        def exp_step(step, mass):
            for u in range(GROUP):
                less = jnp.where(step * GROUP + u < count, 0.0, BIG).astype(F32)
                columns = slice(u * TILE, (u + 1) * TILE)
                term = jnp.exp(score_buf[step, :, columns] - (peak + less))
                score_buf[step, :, columns] = term
                mass = mass + term
            return mass

        mass = lax.fori_loop(0, steps, exp_step, zeros)
        mass = jnp.sum(mass, axis=1, keepdims=True)
        inverse = 1.0 / mass
        log_mass = peak + jnp.log(mass)

        def out_step(step, out):
            probs = (score_buf[step] * inverse).astype(BF16)
            return out + lax.dot_general(probs, keys_of(step), NN, preferred_element_type=F32)

        out = lax.fori_loop(0, steps, out_step, zeros)
        out = out.astype(BF16).astype(F32)
        delta = jnp.sum(jnp.where(low, 0.0, both.astype(F32) * out), axis=1, keepdims=True)

        def grad_step(step, acc):
            keys = keys_of(step)
            prob_grad = lax.dot_general(grad, keys, NT, preferred_element_type=F32)
            score_grad = ((score_buf[step] * inverse) * (prob_grad - delta)).astype(BF16)
            return acc + lax.dot_general(score_grad, keys, NN, preferred_element_type=F32)

        acc = lax.fori_loop(0, steps, grad_step, zeros) * HDIM ** -0.5
        low_part = low_lanes(ROWS // 2)
        for i in range(2):
            top = acc[i * ROWS : i * ROWS + ROWS // 2]
            bottom = acc[i * ROWS + ROWS // 2 : (i + 1) * ROWS]
            dq_ref[2 * t + i] = jnp.where(low_part, top, pltpu.roll(bottom, HDIM, 1)).astype(BF16)
        stats = jnp.where(lane == t, log_mass, stat_buf[...])
        stat_buf[...] = jnp.where(lane == TILES + t, delta, stats)
        return unused

    stat_buf[...] = zeros
    lax.fori_loop(0, TILES, one_tile, 0)
    stat_ref[...] = stat_buf[...].T[:8]


def query_side(kv, qg_own, lists):
    return pl.pallas_call(
        query_kernel,
        name="query_side",
        out_shape=(
            jax.ShapeDtypeStruct((8, LANES), F32),
            jax.ShapeDtypeStruct((2 * TILES, ROWS // 2, LANES), BF16),
        ),
        in_specs=[VMEM_SPEC, VMEM_SPEC, SMEM_SPEC],
        out_specs=(VMEM_SPEC,) * 2,
        scratch_shapes=[
            pltpu.VMEM((SLOTS // GROUP, TILE, GROUP * TILE), F32),
            pltpu.VMEM((TILE, LANES), F32),
        ],
        compiler_params=pltpu.CompilerParams(vmem_limit_bytes=24 * 2**20),
    )(kv.reshape(SLOTS, TILE, LANES), qg_own.reshape(TILES, TILE, LANES), lists)


def key_kernel(qg_ref, stat_ref, kv_own, list_ref, dkv_ref, rows_ref):
    for b in range(BLOCKS):
        for t in range(TILES):
            rows_ref[b * TILES + t, 0:1, :] = stat_ref[b, t : t + 1, :]
            rows_ref[b * TILES + t, 1:2, :] = stat_ref[b, TILES + t : TILES + t + 1, :]
    low = low_lanes(TILE)
    zero = jnp.zeros((TILE, LANES), BF16)

    def one_tile(t, unused):
        count = list_ref[TILES + t, LANES - 1]
        steps = (count + GROUP - 1) // GROUP
        both = kv_own[t]
        stacked = jnp.concatenate([jnp.where(low, both, zero), jnp.where(low, zero, both)], axis=0)

        def step_terms(step, acc):
            lefts, rights = [], []
            for u in range(GROUP):
                slot = list_ref[TILES + t, step * GROUP + u]
                less = jnp.where(step * GROUP + u < count, 0.0, BIG).astype(F32)
                queries = qg_ref[slot]
                products = lax.dot_general(stacked, queries, NT, preferred_element_type=F32)
                probs = jnp.exp(products[:TILE] - (rows_ref[slot, 0:1, :] + less))
                score_grad = probs * (products[TILE:] - rows_ref[slot, 1:2, :])
                lefts += [score_grad.astype(BF16), probs.astype(BF16)]
                rights += [jnp.where(low, queries, zero), jnp.where(low, zero, queries)]
            return acc + lax.dot_general(
                jnp.concatenate(lefts, axis=1), jnp.concatenate(rights, axis=0), NN,
                preferred_element_type=F32,
            )

        acc = lax.fori_loop(0, steps, step_terms, jnp.zeros((TILE, LANES), F32))
        dkv_ref[t] = acc.astype(BF16)
        return unused

    lax.fori_loop(0, TILES, one_tile, 0)


def key_side(qg, stats, kv_own, lists):
    return pl.pallas_call(
        key_kernel,
        name="key_side",
        out_shape=jax.ShapeDtypeStruct((TILES, TILE, LANES), BF16),
        in_specs=[VMEM_SPEC, VMEM_SPEC, VMEM_SPEC, SMEM_SPEC],
        out_specs=VMEM_SPEC,
        scratch_shapes=[
            pltpu.VMEM((SLOTS, 8, LANES), F32),
        ],
        compiler_params=pltpu.CompilerParams(vmem_limit_bytes=24 * 2**20),
    )(qg.reshape(SLOTS, TILE, LANES), stats, kv_own.reshape(TILES, TILE, LANES), lists)


def leave_kernel(dq_ref, dkv_ref, dq_got, dkv_got, pair_send, pair_recv):
    place, core = here()
    wait_all = greet([pair_device(place, core, o) for o in OFFSETS])
    mine = head_of(place, (0, 0, 0))
    sources, landings = (dq_ref, dkv_ref), (dq_got, dkv_got)

    def share_of(offset):
        bits = [(v % 2 + d) % 2 for v, d in zip(place, offset)]
        return (bits[0] * 2 + bits[1]) * 2 + bits[2]

    def pair_copy(which, i, arriving=False):
        landing = landings[which].at[head_of(place, OFFSETS[i]) if arriving else mine]
        return remote(sources[which].at[share_of(OFFSETS[i])], landing,
                      pair_send.at[which, i], pair_recv.at[which, i], pair_device(place, core, OFFSETS[i]))

    wait_all()
    for which in (0, 1):
        for i in range(7):
            pair_copy(which, i).start()
    dq_got[mine] = dq_ref[share_of((0, 0, 0))]
    dkv_got[mine] = dkv_ref[share_of((0, 0, 0))]
    for which in (0, 1):
        for i in range(7):
            pair_copy(which, i, True).wait_recv()
    for which in (0, 1):
        for i in range(7):
            pair_copy(which, i).wait_send()


def unpack_kernel(dq_got, dkv_got, q_ref, k_ref, v_ref, q_out, k_out, v_out, sems):
    def halves(got, j):
        one, two = got[2 * j].astype(F32), got[2 * j + 1].astype(F32)
        low = low_lanes(one.shape[0])
        return (
            jnp.where(low, one, pltpu.roll(two, HDIM, 1)).astype(BF16),
            jnp.where(low, pltpu.roll(one, HDIM, 1), two).astype(BF16),
        )

    for j in range(HEADS // 2):
        columns = slice(j * LANES, (j + 1) * LANES)
        k_out[:, columns], v_out[:, columns] = halves(dkv_got, j)
        q_out[0 : ROWS // 2, columns], q_out[ROWS // 2 : ROWS, columns] = halves(dq_got, j)
    copies = [
        pltpu.make_async_copy(source, target, sems.at[i])
        for i, (source, target) in enumerate([(q_out, q_ref), (k_out, k_ref), (v_out, v_ref)])
    ]
    for copy in copies:
        copy.start()
    for copy in copies:
        copy.wait()


def leave(dq, dkv):
    got = pl.pallas_call(
        leave_kernel,
        name="leave",
        out_shape=(
            jax.ShapeDtypeStruct((HEADS, ROWS // 2, LANES), BF16),
            jax.ShapeDtypeStruct((HEADS, ROWS, LANES), BF16),
        ),
        in_specs=[VMEM_SPEC] * 2,
        out_specs=(VMEM_SPEC,) * 2,
        scratch_shapes=[pltpu.SemaphoreType.DMA((2, 7)), pltpu.SemaphoreType.DMA((2, 7))],
        compiler_params=pltpu.CompilerParams(
            collective_id=2, has_side_effects=True, vmem_limit_bytes=8 * 2**20
        ),
    )(dq, dkv.reshape(HEADS, ROWS, LANES))
    shape = (ROWS, HEADS * HDIM)
    return pl.pallas_call(
        unpack_kernel,
        name="unpack",
        out_shape=(jax.ShapeDtypeStruct(shape, BF16),) * 3,
        in_specs=[VMEM_SPEC] * 2,
        out_specs=(HBM_SPEC,) * 3,
        scratch_shapes=[pltpu.VMEM(shape, BF16)] * 3 + [pltpu.SemaphoreType.DMA((3,))],
        compiler_params=pltpu.CompilerParams(vmem_limit_bytes=8 * 2**20),
    )(*got)


def body(queries, keys, values, out_grad, tile_mask, frame_order):
    kv, qg, kv_own, qg_own, lists = enter(queries, keys, values, out_grad, tile_mask, frame_order)
    stats_own, dq = query_side(kv, qg_own, lists)
    dkv = key_side(qg, share(stats_own), kv_own, lists)
    return leave(dq, dkv)


def solution(mesh):
    whole = P(("blk", "head"), None)
    return jax.shard_map(
        body,
        mesh=mesh,
        in_specs=(whole,) * 4 + (P(), P()),
        out_specs=(whole,) * 3,
        check_vma=False,
    )
```

```python
import functools

import jax
import jax.numpy as jnp
from jax import lax
from jax.experimental import pallas as pl
from jax.experimental.pallas import tpu as pltpu
from jax.sharding import PartitionSpec as P

HDIM = 64
TILE = 128
LANES = 128
HEADS = 8
ROWS = 64
TILES = 4
BLOCK = TILES * TILE
BLOCKS = 16
SLOTS = BLOCKS * TILES
GROUP = 24
KEY_GROUP = 24
SPAN = 4
KEY_SPAN = 4
PIECES = ((0, 176), (176, 176), (352, 160))
MESH = pl.DeviceIdType.MESH
F32 = jnp.float32
BF16 = jnp.bfloat16
BIG = 1e30
NT = (((1,), (1,)), ((), ()))
NN = (((1,), (0,)), ((), ()))
HBM_SPEC = pl.BlockSpec(memory_space=pltpu.HBM)
VMEM_SPEC = pl.BlockSpec(memory_space=pltpu.VMEM)
SMEM_SPEC = pl.BlockSpec(memory_space=pltpu.SMEM)


class Place:
    def __init__(self):
        blk = lax.axis_index("blk")
        z = lax.axis_index("head")
        x = blk // 8
        rest = blk - 8 * x
        y = rest // 2
        self.core = rest - 2 * y
        self.other = 1 - self.core
        self.at = (x, y, z)
        self.high = [(h, 1 - h) for h in (v // 2 for v in self.at)]
        self.low = [(l, 1 - l) for l in (v - 2 * h[0] for v, h in zip(self.at, self.high))]
        halves = [h[0] + l[0] - 2 * h[0] * l[0] for h, l in zip(self.high, self.low)]
        self.half = [(h, 1 - h) for h in halves]
        self.pair = [(v, v + 1 - 2 * l[0]) for v, l in zip(self.at, self.low)]
        self.mirror = [(v, 3 - v) for v in self.at]
        self.known = {}

    def once(self, key, work):
        if key not in self.known:
            self.known[key] = work()
        return self.known[key]

    def device(self, table, offset, flip):
        x, y, z = [t[d] for t, d in zip(table, offset)]
        return ((x * 4 + y) * 2 + (self.other if flip else self.core), z)

    def pair_device(self, offset):
        return self.once(("pair", offset), lambda: self.device(self.pair, offset, 0))

    def mirror_device(self, offset, flip=0):
        return self.once(("mirror", offset, flip), lambda: self.device(self.mirror, offset, flip))

    def number(self, bits, offset):
        return (bits[0][offset[0]] * 2 + bits[1][offset[1]]) * 2 + bits[2][offset[2]]

    def head(self, offset=(0, 0, 0)):
        return self.once(("head", offset), lambda: self.number(self.half, offset))

    def entry(self, offset=(0, 0, 0)):
        return self.once(("entry", offset), lambda: self.number(self.low, offset))

    def block(self, offset=(0, 0, 0), flip=0):
        return self.once(
            ("block", offset, flip),
            lambda: self.number(self.high, offset) * 2 + (self.other if flip else self.core),
        )


ALL_OFFSETS = [(a, b, c) for a in (0, 1) for b in (0, 1) for c in (0, 1)]
OFFSETS = ALL_OFFSETS[1:]


def remote(src, dst, send, recv, target):
    return pltpu.make_async_remote_copy(
        src_ref=src, dst_ref=dst, send_sem=send, recv_sem=recv, device_id=target, device_id_type=MESH
    )


def greet(targets):
    barrier = pltpu.get_barrier_semaphore()
    for target in targets:
        pl.semaphore_signal(barrier, inc=1, device_id=target, device_id_type=MESH)
    return lambda: pl.semaphore_wait(barrier, len(targets))


UNIT = [(1, 0, 0), (0, 1, 0), (0, 0, 1)]


def plus(*offsets):
    return tuple(sum(v) for v in zip(*offsets))


class CubeGather:
    def __init__(self, ref, place, sems):
        self.ref, self.place = ref, place
        self.send, self.recv, self.core_send, self.core_recv = sems
        self.pieces = [0] * len(ALL_OFFSETS)

    def hops(self, piece):
        a1, a2, a3 = [(piece + i) % 3 for i in range(3)]
        u1, u2, o = UNIT[a1], UNIT[a2], (0, 0, 0)
        return [(a1, o), (a2, o), (a2, u1), (a3, o), (a3, u1), (a3, u2), (a3, plus(u1, u2))]

    def hop_copy(self, piece, k, arriving=False):
        axis, offset = self.hops(piece)[k]
        if arriving:
            offset = plus(offset, UNIT[axis])
        first, count = PIECES[piece]
        part = self.ref.at[self.place.block(offset), pl.ds(first, count), :]
        return remote(part, part, self.send.at[piece, k], self.recv.at[piece, k],
                      self.place.mirror_device(UNIT[axis]))

    def core_copy(self, i, arriving=False):
        part = self.ref.at[self.place.block(ALL_OFFSETS[i], int(arriving))]
        return remote(part, part, self.core_send.at[i], self.core_recv.at[i],
                      self.place.mirror_device((0, 0, 0), 1))

    def begin(self):
        for k in (0, 1, 3):
            for p in range(3):
                self.hop_copy(p, k).start()
        self.core_copy(0).start()

    def relay_step(self, k, onward):
        for p in range(3):
            self.hop_copy(p, k, True).wait_recv()
            for j in onward:
                self.hop_copy(p, j).start()
            axis, offset = self.hops(p)[k]
            i = ALL_OFFSETS.index(plus(offset, UNIT[axis]))
            self.pieces[i] += 1
            if self.pieces[i] == 3:
                self.core_copy(i).start()

    def finish(self):
        for i in range(8):
            self.core_copy(i, True).wait_recv()
        for p in range(3):
            for k in range(7):
                self.hop_copy(p, k).wait_send()
        for i in range(8):
            self.core_copy(i).wait_send()


def entry_rows(place, offset=(0, 0, 0)):
    bits = [place.low[a][d] for a, d in enumerate(offset)]
    return pl.ds(pl.multiple_of((bits[0] * 2 + bits[1]) * TILE + bits[2] * ROWS, ROWS), ROWS)


GATHER_SEMS = [
    pltpu.SemaphoreType.DMA((3, 7)),
    pltpu.SemaphoreType.DMA((3, 7)),
    pltpu.SemaphoreType.DMA((8,)),
    pltpu.SemaphoreType.DMA((8,)),
]


def low_lanes(rows):
    return lax.broadcasted_iota(jnp.int32, (rows, LANES), 1) < HDIM


def pack_heads(first_ref, second_ref, packed, scale=None):
    low = low_lanes(ROWS)
    for j in range(HEADS // 2):
        columns = slice(j * LANES, (j + 1) * LANES)
        one = first_ref[:, columns].astype(F32)
        two = second_ref[:, columns].astype(F32)
        if scale is not None:
            one = one * scale
        packed[2 * j] = jnp.where(low, one, pltpu.roll(two, HDIM, 1)).astype(BF16)
        packed[2 * j + 1] = jnp.where(low, pltpu.roll(one, HDIM, 1), two).astype(BF16)


def slot_lists(mask, order, place):
    def dot(a, b, dims=NN):
        return lax.dot_general(a.astype(BF16), b.astype(BF16), dims, preferred_element_type=F32)

    def iota(shape, dim):
        return lax.broadcasted_iota(jnp.int32, shape, dim)

    def one_if(condition):
        return jnp.where(condition, 1.0, 0.0).astype(F32)

    slot = iota((32, SLOTS), 1)
    x = 2 * (slot >> 5) + ((slot >> 1) & 1)
    y = 2 * ((slot >> 4) & 1) + (slot & 1)
    from_frame = one_if((x * 4 + y) * 2 + ((slot >> 2) & 1) == iota((32, SLOTS), 0))
    frames = dot(jnp.broadcast_to(order.astype(F32), (8, 32)), from_frame)
    tiles = (2.0 * frames + ((iota((8, SLOTS), 1) >> 3) & 1).astype(F32))[0:1]
    is_tile = one_if(iota((SLOTS, SLOTS), 0).astype(F32) == tiles)
    row = iota((8, SLOTS), 0)
    is_own = one_if(iota((8, SLOTS), 1) == place.block() * TILES + (row & 3))
    own_tiles = dot(is_own, is_tile, NT)
    mask = one_if(mask == 1)
    attends = dot(dot(own_tiles, mask), is_tile)
    attended = dot(dot(own_tiles, mask, NT), is_tile)
    allowed = jnp.where(row < TILES, attends, attended)
    ahead = dot(allowed, one_if(iota((SLOTS, SLOTS), 0) < iota((SLOTS, SLOTS), 1)))
    count = jnp.sum(allowed, axis=1, keepdims=True)
    ahead = jnp.where(allowed > 0.5, ahead, -1.0)
    place_in_list = iota((LANES, SLOTS), 0).astype(F32)
    slots = iota((8, SLOTS), 1).astype(F32)
    lists = jnp.zeros((8, LANES), F32)
    rows, lanes = iota((8, LANES), 0), iota((8, LANES), 1)
    for r in range(8):
        lists = jnp.where(rows == r, dot(slots, one_if(place_in_list == ahead[r : r + 1]), NT), lists)
    lists = jnp.where(lanes.astype(F32) < count, lists, lists[:, 0:1])
    return jnp.where(lanes == LANES - 1, count, lists).astype(jnp.int32)


def enter_kernel(q_ref, k_ref, v_ref, g_ref, mask_ref, order_ref, kv_ref, qg_ref, kv_own, qg_own, list_ref,
                 q_buf, k_buf, v_buf, g_buf, mask_buf, order_buf, kv_pack, qg_pack, load_sems,
                 pair_send, pair_recv, *gather_sems):
    place = Place()
    wait_all = greet(
        [place.pair_device(o) for o in OFFSETS]
        + [place.mirror_device(u) for u in UNIT]
        + [place.mirror_device((0, 0, 0), 1)]
    )
    loads = [
        pltpu.make_async_copy(source, target, load_sems.at[i])
        for i, (source, target) in enumerate([
            (k_ref, k_buf), (v_ref, v_buf), (q_ref, q_buf), (g_ref, g_buf),
            (mask_ref, mask_buf), (order_ref, order_buf),
        ])
    ]
    for load in loads:
        load.start()
    own = place.block()
    packs, whole = (kv_pack, qg_pack), (kv_ref, qg_ref)

    def pair_copy(which, i, arriving=False):
        rows = entry_rows(place, OFFSETS[i] if arriving else (0, 0, 0))
        return remote(packs[which].at[place.head(OFFSETS[i])], whole[which].at[own, rows, :],
                      pair_send.at[which, i], pair_recv.at[which, i], place.pair_device(OFFSETS[i]))

    def hand_out(which):
        for i in range(7):
            pair_copy(which, i).start()
        here_too = packs[which][place.head()]
        whole[which][own, entry_rows(place), :] = here_too

    gathers = [CubeGather(whole[i], place, gather_sems[4 * i : 4 * i + 4]) for i in range(2)]
    loads[0].wait()
    loads[1].wait()
    pack_heads(k_buf, v_buf, kv_pack)
    wait_all()
    hand_out(0)
    loads[2].wait()
    loads[3].wait()
    pack_heads(q_buf, g_buf, qg_pack, HDIM ** -0.5)
    hand_out(1)
    loads[4].wait()
    loads[5].wait()
    list_ref[...] = slot_lists(mask_buf[...], order_buf[...], place)
    for which in range(2):
        for i in range(7):
            pair_copy(which, i, True).wait_recv()
        gathers[which].begin()
        (kv_own, qg_own)[which][...] = whole[which][own]
    for k, onward in ((0, (2, 4)), (1, (5,)), (2, (6,)), (3, ()), (4, ()), (5, ()), (6, ())):
        for gather in gathers:
            gather.relay_step(k, onward)
    for which in range(2):
        for i in range(7):
            pair_copy(which, i).wait_send()
    for gather in gathers:
        gather.finish()


def enter(q, k, v, g, tile_mask, frame_order):
    entry = pltpu.VMEM((ROWS, HEADS * HDIM), BF16)
    pack = pltpu.VMEM((HEADS, ROWS, LANES), BF16)
    return pl.pallas_call(
        enter_kernel,
        name="enter",
        out_shape=(
            jax.ShapeDtypeStruct((BLOCKS, BLOCK, LANES), BF16),
            jax.ShapeDtypeStruct((BLOCKS, BLOCK, LANES), BF16),
            jax.ShapeDtypeStruct((BLOCK, LANES), BF16),
            jax.ShapeDtypeStruct((BLOCK, LANES), BF16),
            jax.ShapeDtypeStruct((8, LANES), jnp.int32),
        ),
        in_specs=[HBM_SPEC] * 6,
        out_specs=(VMEM_SPEC,) * 5,
        scratch_shapes=[entry] * 4 + [
            pltpu.VMEM(tile_mask.shape, jnp.int32),
            pltpu.VMEM((1, frame_order.shape[0]), jnp.int32),
            pack,
            pack,
            pltpu.SemaphoreType.DMA((6,)),
            pltpu.SemaphoreType.DMA((2, 7)),
            pltpu.SemaphoreType.DMA((2, 7)),
        ] + GATHER_SEMS * 2,
        compiler_params=pltpu.CompilerParams(
            collective_id=0, has_side_effects=True, vmem_limit_bytes=16 * 2**20
        ),
    )(*[pltpu.with_memory_space_constraint(a, pltpu.HBM) for a in (q, k, v, g, tile_mask, frame_order.reshape(1, -1))])


def share_kernel(stat_own, stat_ref, send, recv):
    place = Place()
    peers = [(o, c) for o in ALL_OFFSETS for c in (0, 1)][1:]

    wait_all = greet([place.mirror_device(*p) for p in peers])
    own = place.block()
    stat_ref[own] = stat_own[...]

    def stat_copy(i, arriving=False):
        offset, flip = peers[i]
        source = place.block(offset, flip) if arriving else own
        part = stat_ref.at[source]
        return remote(part, part, send.at[i], recv.at[i], place.mirror_device(offset, flip))

    wait_all()
    for i in range(15):
        stat_copy(i).start()
    for i in range(15):
        stat_copy(i, True).wait_recv()
    for i in range(15):
        stat_copy(i).wait_send()


def share(stat_own):
    return pl.pallas_call(
        share_kernel,
        name="share",
        out_shape=jax.ShapeDtypeStruct((BLOCKS, 8, LANES), F32),
        in_specs=[VMEM_SPEC],
        out_specs=VMEM_SPEC,
        scratch_shapes=[pltpu.SemaphoreType.DMA((15,)), pltpu.SemaphoreType.DMA((15,))],
        compiler_params=pltpu.CompilerParams(
            collective_id=1, has_side_effects=True, vmem_limit_bytes=4 * 2**20
        ),
    )(stat_own)


def query_kernel(kv_ref, qg_own, list_ref, stat_ref, dq_ref, term_buf, peak_buf, stat_buf):
    low = low_lanes(TILE)
    lane = lax.broadcasted_iota(jnp.int32, (TILE, LANES), 1)
    zero = jnp.zeros((TILE, LANES), BF16)
    zeros = jnp.zeros((TILE, LANES), F32)

    def some_tiles(first, unused):
        span = range(SPAN)
        tiles = [first * SPAN + i for i in span]
        counts = [list_ref[t, LANES - 1] for t in tiles]
        most = functools.reduce(jnp.maximum, counts)
        steps = (most + GROUP - 1) // GROUP
        both = [qg_own[t] for t in tiles]

        def keys_of(i, step):
            return jnp.concatenate([kv_ref[list_ref[tiles[i], step * GROUP + u]] for u in range(GROUP)], axis=0)

        def cut(u):
            return slice(u * TILE, (u + 1) * TILE)

        def term_step(step, state):
            after = []
            for i in span:
                before, mass = state[2 * i : 2 * i + 2]
                query = jnp.where(low, both[i], zero)
                scores = lax.dot_general(query, keys_of(i, step), NT, preferred_element_type=F32)
                peak = before
                for u in range(GROUP):
                    peak = jnp.maximum(peak, scores[:, cut(u)])
                mass = mass * jnp.exp(before - peak)
                for u in range(GROUP):
                    less = jnp.where(step * GROUP + u < counts[i], 0.0, BIG).astype(F32)
                    term = jnp.exp(scores[:, cut(u)] - (peak + less))
                    term_buf[i, step, :, cut(u)] = term
                    mass = mass + term
                peak_buf[i, step] = peak
                after += [peak, mass]
            return tuple(after)

        state = lax.fori_loop(0, steps, term_step, (jnp.full((TILE, LANES), -BIG, F32), zeros) * SPAN)
        peaks, inverses, log_masses = [], [], []
        for i in span:
            lane_peak, lane_mass = state[2 * i : 2 * i + 2]
            peak = jnp.max(lane_peak, axis=1, keepdims=True)
            mass = jnp.sum(lane_mass * jnp.exp(lane_peak - peak), axis=1, keepdims=True)
            peaks.append(peak)
            inverses.append(1.0 / mass)
            log_masses.append(peak + jnp.log(mass))

        def out_step(step, outs):
            after = []
            for i in span:
                factor = jnp.exp(peak_buf[i, step] - peaks[i]) * inverses[i]
                peak_buf[i, step] = factor
                probs = [(term_buf[i, step, :, cut(u)] * factor).astype(BF16) for u in range(GROUP)]
                after.append(outs[i] + lax.dot_general(
                    jnp.concatenate(probs, axis=1), keys_of(i, step), NN, preferred_element_type=F32
                ))
            return tuple(after)

        outs = lax.fori_loop(0, steps, out_step, (zeros,) * SPAN)
        deltas = []
        for i in span:
            out = outs[i].astype(BF16).astype(F32)
            deltas.append(jnp.sum(jnp.where(low, 0.0, both[i].astype(F32) * out), axis=1, keepdims=True))

        def grad_step(step, accs):
            after = []
            for i in span:
                keys = keys_of(i, step)
                factor = peak_buf[i, step]
                grad = jnp.where(low, zero, both[i])
                prob_grad = lax.dot_general(grad, keys, NT, preferred_element_type=F32)
                score_grad = [
                    ((term_buf[i, step, :, cut(u)] * factor) * (prob_grad[:, cut(u)] - deltas[i])).astype(BF16)
                    for u in range(GROUP)
                ]
                after.append(accs[i] + lax.dot_general(
                    jnp.concatenate(score_grad, axis=1), keys, NN, preferred_element_type=F32
                ))
            return tuple(after)

        accs = lax.fori_loop(0, steps, grad_step, (zeros,) * SPAN)
        low_part = low_lanes(ROWS // 2)
        stats = stat_buf[...]
        for i in span:
            acc = accs[i] * HDIM ** -0.5
            for j in range(2):
                top = acc[j * ROWS : j * ROWS + ROWS // 2]
                bottom = acc[j * ROWS + ROWS // 2 : (j + 1) * ROWS]
                dq_ref[2 * tiles[i] + j] = jnp.where(low_part, top, pltpu.roll(bottom, HDIM, 1)).astype(BF16)
            stats = jnp.where(lane == tiles[i], log_masses[i], stats)
            stats = jnp.where(lane == TILES + tiles[i], deltas[i], stats)
        stat_buf[...] = stats
        return unused

    stat_buf[...] = zeros
    lax.fori_loop(0, TILES // SPAN, some_tiles, 0)
    stat_ref[...] = stat_buf[...].T[:8]


def query_side(kv, qg_own, lists):
    return pl.pallas_call(
        query_kernel,
        name="query_side",
        out_shape=(
            jax.ShapeDtypeStruct((8, LANES), F32),
            jax.ShapeDtypeStruct((2 * TILES, ROWS // 2, LANES), BF16),
        ),
        in_specs=[VMEM_SPEC, VMEM_SPEC, SMEM_SPEC],
        out_specs=(VMEM_SPEC,) * 2,
        scratch_shapes=[
            pltpu.VMEM((SPAN, -(-SLOTS // GROUP), TILE, GROUP * TILE), F32),
            pltpu.VMEM((SPAN, -(-SLOTS // GROUP), TILE, LANES), F32),
            pltpu.VMEM((TILE, LANES), F32),
        ],
        compiler_params=pltpu.CompilerParams(vmem_limit_bytes=24 * 2**20),
    )(kv.reshape(SLOTS, TILE, LANES), qg_own.reshape(TILES, TILE, LANES), lists)


def key_kernel(qg_ref, stat_ref, kv_own, list_ref, dkv_ref, rows_ref):
    for b in range(BLOCKS):
        for t in range(TILES):
            rows_ref[b * TILES + t, 0:1, :] = stat_ref[b, t : t + 1, :]
            rows_ref[b * TILES + t, 1:2, :] = stat_ref[b, TILES + t : TILES + t + 1, :]
    low = low_lanes(TILE)
    zero = jnp.zeros((TILE, LANES), BF16)

    def some_tiles(first, unused):
        span = range(KEY_SPAN)
        tiles = [first * KEY_SPAN + i for i in span]
        counts = [list_ref[TILES + t, LANES - 1] for t in tiles]
        most = functools.reduce(jnp.maximum, counts)
        steps = (most + KEY_GROUP - 1) // KEY_GROUP
        stacks = [
            jnp.concatenate([jnp.where(low, kv_own[t], zero), jnp.where(low, zero, kv_own[t])], axis=0)
            for t in tiles
        ]

        def step_terms(step, accs):
            after = []
            for i in span:
                lefts, rights = [], []
                for u in range(KEY_GROUP):
                    slot = list_ref[TILES + tiles[i], step * KEY_GROUP + u]
                    less = jnp.where(step * KEY_GROUP + u < counts[i], 0.0, BIG).astype(F32)
                    queries = qg_ref[slot]
                    products = lax.dot_general(stacks[i], queries, NT, preferred_element_type=F32)
                    probs = jnp.exp(products[:TILE] - (rows_ref[slot, 0:1, :] + less))
                    score_grad = probs * (products[TILE:] - rows_ref[slot, 1:2, :])
                    lefts += [score_grad.astype(BF16), probs.astype(BF16)]
                    rights += [jnp.where(low, queries, zero), jnp.where(low, zero, queries)]
                after.append(accs[i] + lax.dot_general(
                    jnp.concatenate(lefts, axis=1), jnp.concatenate(rights, axis=0), NN,
                    preferred_element_type=F32,
                ))
            return tuple(after)

        accs = lax.fori_loop(0, steps, step_terms, (jnp.zeros((TILE, LANES), F32),) * KEY_SPAN)
        for i in span:
            dkv_ref[tiles[i]] = accs[i].astype(BF16)
        return unused

    lax.fori_loop(0, TILES // KEY_SPAN, some_tiles, 0)


def key_side(qg, stats, kv_own, lists):
    return pl.pallas_call(
        key_kernel,
        name="key_side",
        out_shape=jax.ShapeDtypeStruct((TILES, TILE, LANES), BF16),
        in_specs=[VMEM_SPEC, VMEM_SPEC, VMEM_SPEC, SMEM_SPEC],
        out_specs=VMEM_SPEC,
        scratch_shapes=[
            pltpu.VMEM((SLOTS, 8, LANES), F32),
        ],
        compiler_params=pltpu.CompilerParams(vmem_limit_bytes=24 * 2**20),
    )(qg.reshape(SLOTS, TILE, LANES), stats, kv_own.reshape(TILES, TILE, LANES), lists)


def leave_kernel(dq_ref, dkv_ref, dq_got, dkv_got, pair_send, pair_recv):
    place = Place()
    wait_all = greet([place.pair_device(o) for o in OFFSETS])
    mine = place.head()
    sources, landings = (dq_ref, dkv_ref), (dq_got, dkv_got)

    def pair_copy(which, i, arriving=False):
        landing = landings[which].at[place.head(OFFSETS[i]) if arriving else mine]
        return remote(sources[which].at[place.entry(OFFSETS[i])], landing,
                      pair_send.at[which, i], pair_recv.at[which, i], place.pair_device(OFFSETS[i]))

    wait_all()
    for which in (0, 1):
        for i in range(7):
            pair_copy(which, i).start()
    dq_got[mine] = dq_ref[place.entry()]
    dkv_got[mine] = dkv_ref[place.entry()]
    for which in (0, 1):
        for i in range(7):
            pair_copy(which, i, True).wait_recv()
    for which in (0, 1):
        for i in range(7):
            pair_copy(which, i).wait_send()


def unpack_kernel(dq_got, dkv_got, q_ref, k_ref, v_ref, q_out, k_out, v_out, sems):
    def halves(got, j):
        one, two = got[2 * j].astype(F32), got[2 * j + 1].astype(F32)
        low = low_lanes(one.shape[0])
        return (
            jnp.where(low, one, pltpu.roll(two, HDIM, 1)).astype(BF16),
            jnp.where(low, pltpu.roll(one, HDIM, 1), two).astype(BF16),
        )

    for j in range(HEADS // 2):
        columns = slice(j * LANES, (j + 1) * LANES)
        k_out[:, columns], v_out[:, columns] = halves(dkv_got, j)
        q_out[0 : ROWS // 2, columns], q_out[ROWS // 2 : ROWS, columns] = halves(dq_got, j)
    copies = [
        pltpu.make_async_copy(source, target, sems.at[i])
        for i, (source, target) in enumerate([(q_out, q_ref), (k_out, k_ref), (v_out, v_ref)])
    ]
    for copy in copies:
        copy.start()
    for copy in copies:
        copy.wait()


def leave(dq, dkv):
    got = pl.pallas_call(
        leave_kernel,
        name="leave",
        out_shape=(
            jax.ShapeDtypeStruct((HEADS, ROWS // 2, LANES), BF16),
            jax.ShapeDtypeStruct((HEADS, ROWS, LANES), BF16),
        ),
        in_specs=[VMEM_SPEC] * 2,
        out_specs=(VMEM_SPEC,) * 2,
        scratch_shapes=[pltpu.SemaphoreType.DMA((2, 7)), pltpu.SemaphoreType.DMA((2, 7))],
        compiler_params=pltpu.CompilerParams(
            collective_id=2, has_side_effects=True, vmem_limit_bytes=8 * 2**20
        ),
    )(dq, dkv.reshape(HEADS, ROWS, LANES))
    shape = (ROWS, HEADS * HDIM)
    return pl.pallas_call(
        unpack_kernel,
        name="unpack",
        out_shape=(jax.ShapeDtypeStruct(shape, BF16),) * 3,
        in_specs=[VMEM_SPEC] * 2,
        out_specs=(HBM_SPEC,) * 3,
        scratch_shapes=[pltpu.VMEM(shape, BF16)] * 3 + [pltpu.SemaphoreType.DMA((3,))],
        compiler_params=pltpu.CompilerParams(vmem_limit_bytes=8 * 2**20),
    )(*got)


def body(queries, keys, values, out_grad, tile_mask, frame_order):
    kv, qg, kv_own, qg_own, lists = enter(queries, keys, values, out_grad, tile_mask, frame_order)
    stats_own, dq = query_side(kv, qg_own, lists)
    dkv = key_side(qg, share(stats_own), kv_own, lists)
    return leave(dq, dkv)


def solution(mesh):
    whole = P(("blk", "head"), None)
    return jax.shard_map(
        body,
        mesh=mesh,
        in_specs=(whole,) * 4 + (P(), P()),
        out_specs=(whole,) * 3,
        check_vma=False,
    )
```

```python
import functools

import jax
import jax.numpy as jnp
from jax import lax
from jax.experimental import pallas as pl
from jax.experimental.pallas import tpu as pltpu
from jax.sharding import PartitionSpec as P

HDIM = 64
TILE = 128
LANES = 128
HEADS = 8
ROWS = 64
TILES = 4
BLOCK = TILES * TILE
BLOCKS = 16
SLOTS = BLOCKS * TILES
GROUP = 24
KEY_GROUP = 24
SPAN = 4
KEY_SPAN = 4
PIECES = ((0, 176), (176, 176), (352, 160))
MESH = pl.DeviceIdType.MESH
F32 = jnp.float32
BF16 = jnp.bfloat16
BIG = 1e30
NT = (((1,), (1,)), ((), ()))
NN = (((1,), (0,)), ((), ()))
HBM_SPEC = pl.BlockSpec(memory_space=pltpu.HBM)
VMEM_SPEC = pl.BlockSpec(memory_space=pltpu.VMEM)
SMEM_SPEC = pl.BlockSpec(memory_space=pltpu.SMEM)


class Place:
    def __init__(self):
        blk = lax.axis_index("blk")
        z = lax.axis_index("head")
        x = blk // 8
        rest = blk - 8 * x
        y = rest // 2
        self.core = rest - 2 * y
        self.other = 1 - self.core
        self.at = (x, y, z)
        self.high = [(h, 1 - h) for h in (v // 2 for v in self.at)]
        self.low = [(l, 1 - l) for l in (v - 2 * h[0] for v, h in zip(self.at, self.high))]
        halves = [h[0] + l[0] - 2 * h[0] * l[0] for h, l in zip(self.high, self.low)]
        self.half = [(h, 1 - h) for h in halves]
        self.pair = [(v, v + 1 - 2 * l[0]) for v, l in zip(self.at, self.low)]
        self.mirror = [(v, 3 - v) for v in self.at]
        self.known = {}

    def once(self, key, work):
        if key not in self.known:
            self.known[key] = work()
        return self.known[key]

    def device(self, table, offset, flip):
        x, y, z = [t[d] for t, d in zip(table, offset)]
        return ((x * 4 + y) * 2 + (self.other if flip else self.core), z)

    def pair_device(self, offset):
        return self.once(("pair", offset), lambda: self.device(self.pair, offset, 0))

    def mirror_device(self, offset, flip=0):
        return self.once(("mirror", offset, flip), lambda: self.device(self.mirror, offset, flip))

    def number(self, bits, offset):
        return (bits[0][offset[0]] * 2 + bits[1][offset[1]]) * 2 + bits[2][offset[2]]

    def head(self, offset=(0, 0, 0)):
        return self.once(("head", offset), lambda: self.number(self.half, offset))

    def entry(self, offset=(0, 0, 0)):
        return self.once(("entry", offset), lambda: self.number(self.low, offset))

    def block(self, offset=(0, 0, 0), flip=0):
        return self.once(
            ("block", offset, flip),
            lambda: self.number(self.high, offset) * 2 + (self.other if flip else self.core),
        )


ALL_OFFSETS = [(a, b, c) for a in (0, 1) for b in (0, 1) for c in (0, 1)]
OFFSETS = sorted(ALL_OFFSETS[1:], key=sum, reverse=True)


def remote(src, dst, send, recv, target):
    return pltpu.make_async_remote_copy(
        src_ref=src, dst_ref=dst, send_sem=send, recv_sem=recv, device_id=target, device_id_type=MESH
    )


def greet(targets):
    barrier = pltpu.get_barrier_semaphore()
    for target in targets:
        pl.semaphore_signal(barrier, inc=1, device_id=target, device_id_type=MESH)
    return lambda: pl.semaphore_wait(barrier, len(targets))


UNIT = [(1, 0, 0), (0, 1, 0), (0, 0, 1)]


def plus(*offsets):
    return tuple(sum(v) for v in zip(*offsets))


class CubeGather:
    def __init__(self, ref, place, sems):
        self.ref, self.place = ref, place
        self.forward = len(sems) == 4
        self.send, self.recv = sems[:2]
        if self.forward:
            self.core_send, self.core_recv = sems[2:]
        self.pieces = [0] * len(ALL_OFFSETS)

    def hops(self, piece):
        a1, a2, a3 = [(piece + i) % 3 for i in range(3)]
        u1, u2, o = UNIT[a1], UNIT[a2], (0, 0, 0)
        return [(a1, o), (a2, o), (a2, u1), (a3, o), (a3, u1), (a3, u2), (a3, plus(u1, u2))]

    def hop_copy(self, piece, k, arriving=False):
        axis, offset = self.hops(piece)[k]
        if arriving:
            offset = plus(offset, UNIT[axis])
        first, count = PIECES[piece]
        part = self.ref.at[self.place.block(offset), pl.ds(first, count), :]
        return remote(part, part, self.send.at[piece, k], self.recv.at[piece, k],
                      self.place.mirror_device(UNIT[axis]))

    def core_copy(self, i, arriving=False):
        part = self.ref.at[self.place.block(ALL_OFFSETS[i], int(arriving))]
        return remote(part, part, self.core_send.at[i], self.core_recv.at[i],
                      self.place.mirror_device((0, 0, 0), 1))

    def begin(self):
        for k in (0, 1, 3):
            for p in range(3):
                self.hop_copy(p, k).start()
        if self.forward:
            self.core_copy(0).start()

    def relay_step(self, k, onward):
        for p in range(3):
            self.hop_copy(p, k, True).wait_recv()
            for j in onward:
                self.hop_copy(p, j).start()
            axis, offset = self.hops(p)[k]
            i = ALL_OFFSETS.index(plus(offset, UNIT[axis]))
            self.pieces[i] += 1
            if self.forward and self.pieces[i] == 3:
                self.core_copy(i).start()

    def finish(self):
        if self.forward:
            for i in range(8):
                self.core_copy(i, True).wait_recv()
        for p in range(3):
            for k in range(7):
                self.hop_copy(p, k).wait_send()
        if self.forward:
            for i in range(8):
                self.core_copy(i).wait_send()


def entry_rows(place, offset=(0, 0, 0)):
    bits = [place.low[a][d] for a, d in enumerate(offset)]
    return pl.ds(pl.multiple_of((bits[0] * 2 + bits[1]) * TILE + bits[2] * ROWS, ROWS), ROWS)


GATHER_SEMS = [
    pltpu.SemaphoreType.DMA((3, 7)),
    pltpu.SemaphoreType.DMA((3, 7)),
    pltpu.SemaphoreType.DMA((8,)),
    pltpu.SemaphoreType.DMA((8,)),
]


def low_lanes(rows):
    return lax.broadcasted_iota(jnp.int32, (rows, LANES), 1) < HDIM


def pack_heads(first_ref, second_ref, packed, scale=None):
    low = low_lanes(ROWS)
    for j in range(HEADS // 2):
        columns = slice(j * LANES, (j + 1) * LANES)
        one = first_ref[:, columns].astype(F32)
        two = second_ref[:, columns].astype(F32)
        if scale is not None:
            one = one * scale
        packed[2 * j] = jnp.where(low, one, pltpu.roll(two, HDIM, 1)).astype(BF16)
        packed[2 * j + 1] = jnp.where(low, pltpu.roll(one, HDIM, 1), two).astype(BF16)


def slot_lists(mask, order, place):
    def dot(a, b, dims=NN):
        return lax.dot_general(a.astype(BF16), b.astype(BF16), dims, preferred_element_type=F32)

    def iota(shape, dim):
        return lax.broadcasted_iota(jnp.int32, shape, dim)

    def one_if(condition):
        return jnp.where(condition, 1.0, 0.0).astype(F32)

    slot = iota((32, SLOTS), 1)
    x = 2 * (slot >> 5) + ((slot >> 1) & 1)
    y = 2 * ((slot >> 4) & 1) + (slot & 1)
    from_frame = one_if((x * 4 + y) * 2 + ((slot >> 2) & 1) == iota((32, SLOTS), 0))
    frames = dot(jnp.broadcast_to(order.astype(F32), (8, 32)), from_frame)
    tiles = (2.0 * frames + ((iota((8, SLOTS), 1) >> 3) & 1).astype(F32))[0:1]
    is_tile = one_if(iota((SLOTS, SLOTS), 0).astype(F32) == tiles)
    row = iota((8, SLOTS), 0)
    is_own = one_if(iota((8, SLOTS), 1) == place.block() * TILES + (row & 3))
    own_tiles = dot(is_own, is_tile, NT)
    mask = one_if(mask == 1)
    attends = dot(dot(own_tiles, mask), is_tile)
    attended = dot(dot(own_tiles, mask, NT), is_tile)
    allowed = jnp.where(row < TILES, attends, attended)
    ahead = dot(allowed, one_if(iota((SLOTS, SLOTS), 0) < iota((SLOTS, SLOTS), 1)))
    count = jnp.sum(allowed, axis=1, keepdims=True)
    ahead = jnp.where(allowed > 0.5, ahead, -1.0)
    place_in_list = iota((LANES, SLOTS), 0).astype(F32)
    slots = iota((8, SLOTS), 1).astype(F32)
    lists = jnp.zeros((8, LANES), F32)
    rows, lanes = iota((8, LANES), 0), iota((8, LANES), 1)
    for r in range(8):
        lists = jnp.where(rows == r, dot(slots, one_if(place_in_list == ahead[r : r + 1]), NT), lists)
    lists = jnp.where(lanes.astype(F32) < count, lists, lists[:, 0:1])
    return jnp.where(lanes == LANES - 1, count, lists).astype(jnp.int32)


def enter_kernel(q_ref, k_ref, v_ref, g_ref, mask_ref, order_ref, kv_ref, qg_ref, kv_own, qg_own, list_ref,
                 q_buf, k_buf, v_buf, g_buf, mask_buf, order_buf, kv_pack, qg_pack, load_sems,
                 pair_send, pair_recv, *gather_sems):
    place = Place()
    wait_all = greet(
        [place.pair_device(o) for o in OFFSETS]
        + [place.mirror_device(u) for u in UNIT]
        + [place.mirror_device((0, 0, 0), 1)]
    )
    loads = [
        pltpu.make_async_copy(source, target, load_sems.at[i])
        for i, (source, target) in enumerate([
            (k_ref, k_buf), (v_ref, v_buf), (q_ref, q_buf), (g_ref, g_buf),
            (mask_ref, mask_buf), (order_ref, order_buf),
        ])
    ]
    for load in loads:
        load.start()
    own = place.block()
    packs, landings = (kv_pack, qg_pack), (kv_ref.at[own], qg_ref.at[own])

    def pair_copy(which, i, arriving=False):
        rows = entry_rows(place, OFFSETS[i] if arriving else (0, 0, 0))
        return remote(packs[which].at[place.head(OFFSETS[i])], landings[which].at[rows, :],
                      pair_send.at[which, i], pair_recv.at[which, i], place.pair_device(OFFSETS[i]))

    def hand_out(which):
        for i in range(7):
            pair_copy(which, i).start()
        here_too = packs[which][place.head()]
        landings[which][entry_rows(place), :] = here_too

    def taken_in(which):
        for i in range(7):
            pair_copy(which, i, True).wait_recv()

    gathers = [CubeGather(kv_ref, place, gather_sems[:4]), CubeGather(qg_ref, place, gather_sems[4:])]
    loads[0].wait()
    loads[1].wait()
    pack_heads(k_buf, v_buf, kv_pack)
    wait_all()
    hand_out(0)
    loads[2].wait()
    loads[3].wait()
    pack_heads(q_buf, g_buf, qg_pack, HDIM ** -0.5)
    hand_out(1)
    loads[4].wait()
    loads[5].wait()
    list_ref[...] = slot_lists(mask_buf[...], order_buf[...], place)
    for which in range(2):
        taken_in(which)
        gathers[which].begin()
        (kv_own, qg_own)[which][...] = landings[which][...]
    for k, onward in ((0, (2, 4)), (1, (5,)), (2, (6,)), (3, ()), (4, ()), (5, ()), (6, ())):
        for gather in gathers:
            gather.relay_step(k, onward)
    for which in range(2):
        for i in range(7):
            pair_copy(which, i).wait_send()
    for gather in gathers:
        gather.finish()


def enter(q, k, v, g, tile_mask, frame_order):
    entry = pltpu.VMEM((ROWS, HEADS * HDIM), BF16)
    pack = pltpu.VMEM((HEADS, ROWS, LANES), BF16)
    return pl.pallas_call(
        enter_kernel,
        name="enter",
        out_shape=(
            jax.ShapeDtypeStruct((BLOCKS, BLOCK, LANES), BF16),
            jax.ShapeDtypeStruct((BLOCKS, BLOCK, LANES), BF16),
            jax.ShapeDtypeStruct((BLOCK, LANES), BF16),
            jax.ShapeDtypeStruct((BLOCK, LANES), BF16),
            jax.ShapeDtypeStruct((8, LANES), jnp.int32),
        ),
        in_specs=[HBM_SPEC] * 6,
        out_specs=(VMEM_SPEC,) * 5,
        scratch_shapes=[entry] * 4 + [
            pltpu.VMEM(tile_mask.shape, jnp.int32),
            pltpu.VMEM((1, frame_order.shape[0]), jnp.int32),
            pack,
            pack,
            pltpu.SemaphoreType.DMA((6,)),
            pltpu.SemaphoreType.DMA((2, 7)),
            pltpu.SemaphoreType.DMA((2, 7)),
        ] + GATHER_SEMS + GATHER_SEMS[:2],
        compiler_params=pltpu.CompilerParams(
            collective_id=0, has_side_effects=True, vmem_limit_bytes=16 * 2**20
        ),
    )(*[pltpu.with_memory_space_constraint(a, pltpu.HBM) for a in (q, k, v, g, tile_mask, frame_order.reshape(1, -1))])


def share_kernel(qg_mine, stat_own, dq_ref, qg_ref, stat_ref, dq_got, stat_send, stat_recv, pair_send, pair_recv,
                 core_send, core_recv):
    place = Place()
    peers = [(o, c) for o in OFFSETS for c in (0, 1)] + [((0, 0, 0), 1)]
    wait_all = greet(
        [place.mirror_device(*p) for p in peers] + [place.pair_device(o) for o in OFFSETS]
    )
    own = place.block()
    stat_ref[own] = stat_own[...]
    for offset in ALL_OFFSETS:
        qg_ref[place.block(offset)] = qg_mine[place.block(offset)]

    def core_copy(i, arriving=False):
        block = place.block(ALL_OFFSETS[i], int(arriving))
        return remote(qg_mine.at[block], qg_ref.at[block], core_send.at[i], core_recv.at[i],
                      place.mirror_device((0, 0, 0), 1))

    def stat_copy(i, arriving=False):
        offset, flip = peers[i]
        source = place.block(offset, flip) if arriving else own
        part = stat_ref.at[source]
        return remote(part, part, stat_send.at[i], stat_recv.at[i], place.mirror_device(offset, flip))

    def pair_copy(i, arriving=False):
        landing = dq_got.at[place.head(OFFSETS[i]) if arriving else place.head()]
        return remote(dq_ref.at[place.entry(OFFSETS[i])], landing, pair_send.at[i], pair_recv.at[i],
                      place.pair_device(OFFSETS[i]))

    wait_all()
    for i in range(15):
        stat_copy(i).start()
    for i in range(7):
        pair_copy(i).start()
    for i in range(8):
        core_copy(i).start()
    dq_got[place.head()] = dq_ref[place.entry()]
    for i in range(8):
        core_copy(i, True).wait_recv()
    for i in range(15):
        stat_copy(i, True).wait_recv()
    for i in range(7):
        pair_copy(i, True).wait_recv()
    for i in range(8):
        core_copy(i).wait_send()
    for i in range(15):
        stat_copy(i).wait_send()
    for i in range(7):
        pair_copy(i).wait_send()


def share(qg_mine, stat_own, dq):
    return pl.pallas_call(
        share_kernel,
        name="share",
        out_shape=(
            jax.ShapeDtypeStruct((BLOCKS, BLOCK, LANES), BF16),
            jax.ShapeDtypeStruct((BLOCKS, 8, LANES), F32),
            jax.ShapeDtypeStruct((HEADS, ROWS // 2, LANES), BF16),
        ),
        in_specs=[VMEM_SPEC] * 3,
        out_specs=(VMEM_SPEC,) * 3,
        scratch_shapes=[
            pltpu.SemaphoreType.DMA((15,)),
            pltpu.SemaphoreType.DMA((15,)),
            pltpu.SemaphoreType.DMA((7,)),
            pltpu.SemaphoreType.DMA((7,)),
            pltpu.SemaphoreType.DMA((8,)),
            pltpu.SemaphoreType.DMA((8,)),
        ],
        compiler_params=pltpu.CompilerParams(
            collective_id=1, has_side_effects=True, vmem_limit_bytes=8 * 2**20
        ),
    )(qg_mine, stat_own, dq)


def query_kernel(kv_ref, qg_own, list_ref, stat_ref, dq_ref, term_buf, peak_buf, stat_buf):
    low = low_lanes(TILE)
    lane = lax.broadcasted_iota(jnp.int32, (TILE, LANES), 1)
    zero = jnp.zeros((TILE, LANES), BF16)
    zeros = jnp.zeros((TILE, LANES), F32)

    def some_tiles(first, unused):
        span = range(SPAN)
        tiles = [first * SPAN + i for i in span]
        counts = [list_ref[t, LANES - 1] for t in tiles]
        most = functools.reduce(jnp.maximum, counts)
        steps = (most + GROUP - 1) // GROUP
        both = [qg_own[t] for t in tiles]

        def keys_of(i, step):
            return jnp.concatenate([kv_ref[list_ref[tiles[i], step * GROUP + u]] for u in range(GROUP)], axis=0)

        def cut(u):
            return slice(u * TILE, (u + 1) * TILE)

        def term_step(step, state):
            after = []
            for i in span:
                before, mass = state[2 * i : 2 * i + 2]
                query = jnp.where(low, both[i], zero)
                scores = lax.dot_general(query, keys_of(i, step), NT, preferred_element_type=F32)
                peak = before
                for u in range(GROUP):
                    peak = jnp.maximum(peak, scores[:, cut(u)])
                mass = mass * jnp.exp(before - peak)
                for u in range(GROUP):
                    less = jnp.where(step * GROUP + u < counts[i], 0.0, BIG).astype(F32)
                    term = jnp.exp(scores[:, cut(u)] - (peak + less))
                    term_buf[i, step, :, cut(u)] = term
                    mass = mass + term
                peak_buf[i, step] = peak
                after += [peak, mass]
            return tuple(after)

        state = lax.fori_loop(0, steps, term_step, (jnp.full((TILE, LANES), -BIG, F32), zeros) * SPAN)
        peaks, inverses, log_masses = [], [], []
        for i in span:
            lane_peak, lane_mass = state[2 * i : 2 * i + 2]
            peak = jnp.max(lane_peak, axis=1, keepdims=True)
            mass = jnp.sum(lane_mass * jnp.exp(lane_peak - peak), axis=1, keepdims=True)
            peaks.append(peak)
            inverses.append(1.0 / mass)
            log_masses.append(peak + jnp.log(mass))

        def out_step(step, outs):
            after = []
            for i in span:
                factor = jnp.exp(peak_buf[i, step] - peaks[i]) * inverses[i]
                peak_buf[i, step] = factor
                probs = [(term_buf[i, step, :, cut(u)] * factor).astype(BF16) for u in range(GROUP)]
                after.append(outs[i] + lax.dot_general(
                    jnp.concatenate(probs, axis=1), keys_of(i, step), NN, preferred_element_type=F32
                ))
            return tuple(after)

        outs = lax.fori_loop(0, steps, out_step, (zeros,) * SPAN)
        deltas = []
        for i in span:
            out = outs[i].astype(BF16).astype(F32)
            deltas.append(jnp.sum(jnp.where(low, 0.0, both[i].astype(F32) * out), axis=1, keepdims=True))

        def grad_step(step, accs):
            after = []
            for i in span:
                keys = keys_of(i, step)
                factor = peak_buf[i, step]
                grad = jnp.where(low, zero, both[i])
                prob_grad = lax.dot_general(grad, keys, NT, preferred_element_type=F32)
                score_grad = [
                    ((term_buf[i, step, :, cut(u)] * factor) * (prob_grad[:, cut(u)] - deltas[i])).astype(BF16)
                    for u in range(GROUP)
                ]
                after.append(accs[i] + lax.dot_general(
                    jnp.concatenate(score_grad, axis=1), keys, NN, preferred_element_type=F32
                ))
            return tuple(after)

        accs = lax.fori_loop(0, steps, grad_step, (zeros,) * SPAN)
        low_part = low_lanes(ROWS // 2)
        stats = stat_buf[...]
        for i in span:
            acc = accs[i] * HDIM ** -0.5
            for j in range(2):
                top = acc[j * ROWS : j * ROWS + ROWS // 2]
                bottom = acc[j * ROWS + ROWS // 2 : (j + 1) * ROWS]
                dq_ref[2 * tiles[i] + j] = jnp.where(low_part, top, pltpu.roll(bottom, HDIM, 1)).astype(BF16)
            stats = jnp.where(lane == tiles[i], log_masses[i], stats)
            stats = jnp.where(lane == TILES + tiles[i], deltas[i], stats)
        stat_buf[...] = stats
        return unused

    stat_buf[...] = zeros
    lax.fori_loop(0, TILES // SPAN, some_tiles, 0)
    stat_ref[...] = stat_buf[...].T[:8]


def query_side(kv, qg_own, lists):
    return pl.pallas_call(
        query_kernel,
        name="query_side",
        out_shape=(
            jax.ShapeDtypeStruct((8, LANES), F32),
            jax.ShapeDtypeStruct((2 * TILES, ROWS // 2, LANES), BF16),
        ),
        in_specs=[VMEM_SPEC, VMEM_SPEC, SMEM_SPEC],
        out_specs=(VMEM_SPEC,) * 2,
        scratch_shapes=[
            pltpu.VMEM((SPAN, -(-SLOTS // GROUP), TILE, GROUP * TILE), F32),
            pltpu.VMEM((SPAN, -(-SLOTS // GROUP), TILE, LANES), F32),
            pltpu.VMEM((TILE, LANES), F32),
        ],
        compiler_params=pltpu.CompilerParams(vmem_limit_bytes=24 * 2**20),
    )(kv.reshape(SLOTS, TILE, LANES), qg_own.reshape(TILES, TILE, LANES), lists)


def key_kernel(qg_ref, stat_ref, kv_own, list_ref, dkv_ref, rows_ref):
    for b in range(BLOCKS):
        for t in range(TILES):
            rows_ref[b * TILES + t, 0:1, :] = stat_ref[b, t : t + 1, :]
            rows_ref[b * TILES + t, 1:2, :] = stat_ref[b, TILES + t : TILES + t + 1, :]
    low = low_lanes(TILE)
    zero = jnp.zeros((TILE, LANES), BF16)

    def some_tiles(first, unused):
        span = range(KEY_SPAN)
        tiles = [first * KEY_SPAN + i for i in span]
        counts = [list_ref[TILES + t, LANES - 1] for t in tiles]
        most = functools.reduce(jnp.maximum, counts)
        steps = (most + KEY_GROUP - 1) // KEY_GROUP
        stacks = [
            jnp.concatenate([jnp.where(low, kv_own[t], zero), jnp.where(low, zero, kv_own[t])], axis=0)
            for t in tiles
        ]

        def step_terms(step, accs):
            after = []
            for i in span:
                lefts, rights = [], []
                for u in range(KEY_GROUP):
                    slot = list_ref[TILES + tiles[i], step * KEY_GROUP + u]
                    less = jnp.where(step * KEY_GROUP + u < counts[i], 0.0, BIG).astype(F32)
                    queries = qg_ref[slot]
                    products = lax.dot_general(stacks[i], queries, NT, preferred_element_type=F32)
                    probs = jnp.exp(products[:TILE] - (rows_ref[slot, 0:1, :] + less))
                    score_grad = probs * (products[TILE:] - rows_ref[slot, 1:2, :])
                    lefts += [score_grad.astype(BF16), probs.astype(BF16)]
                    rights += [jnp.where(low, queries, zero), jnp.where(low, zero, queries)]
                after.append(accs[i] + lax.dot_general(
                    jnp.concatenate(lefts, axis=1), jnp.concatenate(rights, axis=0), NN,
                    preferred_element_type=F32,
                ))
            return tuple(after)

        accs = lax.fori_loop(0, steps, step_terms, (jnp.zeros((TILE, LANES), F32),) * KEY_SPAN)
        for i in span:
            dkv_ref[tiles[i]] = accs[i].astype(BF16)
        return unused

    lax.fori_loop(0, TILES // KEY_SPAN, some_tiles, 0)


def key_side(qg, stats, kv_own, lists):
    return pl.pallas_call(
        key_kernel,
        name="key_side",
        out_shape=jax.ShapeDtypeStruct((TILES, TILE, LANES), BF16),
        in_specs=[VMEM_SPEC, VMEM_SPEC, VMEM_SPEC, SMEM_SPEC],
        out_specs=VMEM_SPEC,
        scratch_shapes=[
            pltpu.VMEM((SLOTS, 8, LANES), F32),
        ],
        compiler_params=pltpu.CompilerParams(vmem_limit_bytes=24 * 2**20),
    )(qg.reshape(SLOTS, TILE, LANES), stats, kv_own.reshape(TILES, TILE, LANES), lists)


def leave_kernel(dkv_ref, dkv_got, pair_send, pair_recv):
    place = Place()
    wait_all = greet([place.pair_device(o) for o in OFFSETS])

    def pair_copy(i, arriving=False):
        landing = dkv_got.at[place.head(OFFSETS[i]) if arriving else place.head()]
        return remote(dkv_ref.at[place.entry(OFFSETS[i])], landing, pair_send.at[i], pair_recv.at[i],
                      place.pair_device(OFFSETS[i]))

    wait_all()
    for i in range(7):
        pair_copy(i).start()
    dkv_got[place.head()] = dkv_ref[place.entry()]
    for i in range(7):
        pair_copy(i, True).wait_recv()
    for i in range(7):
        pair_copy(i).wait_send()


def unpack_kernel(dq_got, dkv_got, q_ref, k_ref, v_ref, q_out, k_out, v_out, sems):
    def halves(got, j):
        one, two = got[2 * j].astype(F32), got[2 * j + 1].astype(F32)
        low = low_lanes(one.shape[0])
        return (
            jnp.where(low, one, pltpu.roll(two, HDIM, 1)).astype(BF16),
            jnp.where(low, pltpu.roll(one, HDIM, 1), two).astype(BF16),
        )

    for j in range(HEADS // 2):
        columns = slice(j * LANES, (j + 1) * LANES)
        k_out[:, columns], v_out[:, columns] = halves(dkv_got, j)
        q_out[0 : ROWS // 2, columns], q_out[ROWS // 2 : ROWS, columns] = halves(dq_got, j)
    copies = [
        pltpu.make_async_copy(source, target, sems.at[i])
        for i, (source, target) in enumerate([(q_out, q_ref), (k_out, k_ref), (v_out, v_ref)])
    ]
    for copy in copies:
        copy.start()
    for copy in copies:
        copy.wait()


def leave(dq_got, dkv):
    dkv_got = pl.pallas_call(
        leave_kernel,
        name="leave",
        out_shape=jax.ShapeDtypeStruct((HEADS, ROWS, LANES), BF16),
        in_specs=[VMEM_SPEC],
        out_specs=VMEM_SPEC,
        scratch_shapes=[pltpu.SemaphoreType.DMA((7,)), pltpu.SemaphoreType.DMA((7,))],
        compiler_params=pltpu.CompilerParams(
            collective_id=2, has_side_effects=True, vmem_limit_bytes=8 * 2**20
        ),
    )(dkv.reshape(HEADS, ROWS, LANES))
    shape = (ROWS, HEADS * HDIM)
    return pl.pallas_call(
        unpack_kernel,
        name="unpack",
        out_shape=(jax.ShapeDtypeStruct(shape, BF16),) * 3,
        in_specs=[VMEM_SPEC] * 2,
        out_specs=(HBM_SPEC,) * 3,
        scratch_shapes=[pltpu.VMEM(shape, BF16)] * 3 + [pltpu.SemaphoreType.DMA((3,))],
        compiler_params=pltpu.CompilerParams(vmem_limit_bytes=8 * 2**20),
    )(dq_got, dkv_got)


def body(queries, keys, values, out_grad, tile_mask, frame_order):
    kv, qg_mine, kv_own, qg_own, lists = enter(queries, keys, values, out_grad, tile_mask, frame_order)
    stats_own, dq = query_side(kv, qg_own, lists)
    qg, stats, dq_got = share(qg_mine, stats_own, dq)
    return leave(dq_got, key_side(qg, stats, kv_own, lists))


def solution(mesh):
    whole = P(("blk", "head"), None)
    return jax.shard_map(
        body,
        mesh=mesh,
        in_specs=(whole,) * 4 + (P(), P()),
        out_specs=(whole,) * 3,
        check_vma=False,
    )
```

```python
import functools

import jax
import jax.numpy as jnp
from jax import lax
from jax.experimental import pallas as pl
from jax.experimental.pallas import tpu as pltpu
from jax.sharding import PartitionSpec as P

HDIM = 64
TILE = 128
LANES = 128
HEADS = 8
ROWS = 64
TILES = 4
BLOCK = TILES * TILE
BLOCKS = 16
SLOTS = BLOCKS * TILES
FIRST = 24
GROUP = 8
KEY_GROUP = 8
SPAN = 4
KEY_SPAN = 4
PIECES = ((0, 176), (176, 176), (352, 160))
MESH = pl.DeviceIdType.MESH
F32 = jnp.float32
BF16 = jnp.bfloat16
BIG = 1e30
NT = (((1,), (1,)), ((), ()))
NN = (((1,), (0,)), ((), ()))
HBM_SPEC = pl.BlockSpec(memory_space=pltpu.HBM)
VMEM_SPEC = pl.BlockSpec(memory_space=pltpu.VMEM)
SMEM_SPEC = pl.BlockSpec(memory_space=pltpu.SMEM)


class Place:
    def __init__(self):
        blk = lax.axis_index("blk")
        z = lax.axis_index("head")
        x = blk // 8
        rest = blk - 8 * x
        y = rest // 2
        self.core = rest - 2 * y
        self.other = 1 - self.core
        self.at = (x, y, z)
        self.high = [(h, 1 - h) for h in (v // 2 for v in self.at)]
        self.low = [(l, 1 - l) for l in (v - 2 * h[0] for v, h in zip(self.at, self.high))]
        halves = [h[0] + l[0] - 2 * h[0] * l[0] for h, l in zip(self.high, self.low)]
        self.half = [(h, 1 - h) for h in halves]
        self.pair = [(v, v + 1 - 2 * l[0]) for v, l in zip(self.at, self.low)]
        self.mirror = [(v, 3 - v) for v in self.at]
        self.known = {}

    def once(self, key, work):
        if key not in self.known:
            self.known[key] = work()
        return self.known[key]

    def device(self, table, offset, flip):
        x, y, z = [t[d] for t, d in zip(table, offset)]
        return ((x * 4 + y) * 2 + (self.other if flip else self.core), z)

    def pair_device(self, offset):
        return self.once(("pair", offset), lambda: self.device(self.pair, offset, 0))

    def mirror_device(self, offset, flip=0):
        return self.once(("mirror", offset, flip), lambda: self.device(self.mirror, offset, flip))

    def number(self, bits, offset):
        return (bits[0][offset[0]] * 2 + bits[1][offset[1]]) * 2 + bits[2][offset[2]]

    def head(self, offset=(0, 0, 0)):
        return self.once(("head", offset), lambda: self.number(self.half, offset))

    def entry(self, offset=(0, 0, 0)):
        return self.once(("entry", offset), lambda: self.number(self.low, offset))

    def block(self, offset=(0, 0, 0), flip=0):
        return self.once(
            ("block", offset, flip),
            lambda: self.number(self.high, offset) * 2 + (self.other if flip else self.core),
        )


ALL_OFFSETS = [(a, b, c) for a in (0, 1) for b in (0, 1) for c in (0, 1)]
OFFSETS = sorted(ALL_OFFSETS[1:], key=sum, reverse=True)


def remote(src, dst, send, recv, target):
    return pltpu.make_async_remote_copy(
        src_ref=src, dst_ref=dst, send_sem=send, recv_sem=recv, device_id=target, device_id_type=MESH
    )


def greet(targets):
    barrier = pltpu.get_barrier_semaphore()
    for target in targets:
        pl.semaphore_signal(barrier, inc=1, device_id=target, device_id_type=MESH)
    return lambda: pl.semaphore_wait(barrier, len(targets))


UNIT = [(1, 0, 0), (0, 1, 0), (0, 0, 1)]


def plus(*offsets):
    return tuple(sum(v) for v in zip(*offsets))


class CubeGather:
    def __init__(self, ref, place, sems):
        self.ref, self.place = ref, place
        self.forward = len(sems) == 4
        self.send, self.recv = sems[:2]
        if self.forward:
            self.core_send, self.core_recv = sems[2:]
        self.pieces = [0] * len(ALL_OFFSETS)

    def hops(self, piece):
        a1, a2, a3 = [(piece + i) % 3 for i in range(3)]
        u1, u2, o = UNIT[a1], UNIT[a2], (0, 0, 0)
        return [(a1, o), (a2, o), (a2, u1), (a3, o), (a3, u1), (a3, u2), (a3, plus(u1, u2))]

    def hop_copy(self, piece, k, arriving=False):
        axis, offset = self.hops(piece)[k]
        if arriving:
            offset = plus(offset, UNIT[axis])
        first, count = PIECES[piece]
        part = self.ref.at[self.place.block(offset), pl.ds(first, count), :]
        return remote(part, part, self.send.at[piece, k], self.recv.at[piece, k],
                      self.place.mirror_device(UNIT[axis]))

    def core_copy(self, i, arriving=False):
        part = self.ref.at[self.place.block(ALL_OFFSETS[i], int(arriving))]
        return remote(part, part, self.core_send.at[i], self.core_recv.at[i],
                      self.place.mirror_device((0, 0, 0), 1))

    def begin(self):
        for k in (0, 1, 3):
            for p in range(3):
                self.hop_copy(p, k).start()
        if self.forward:
            self.core_copy(0).start()

    def relay_step(self, k, onward):
        for p in range(3):
            self.hop_copy(p, k, True).wait_recv()
            for j in onward:
                self.hop_copy(p, j).start()
            axis, offset = self.hops(p)[k]
            i = ALL_OFFSETS.index(plus(offset, UNIT[axis]))
            self.pieces[i] += 1
            if self.forward and self.pieces[i] == 3:
                self.core_copy(i).start()

    def finish(self):
        if self.forward:
            for i in range(8):
                self.core_copy(i, True).wait_recv()
        for p in range(3):
            for k in range(7):
                self.hop_copy(p, k).wait_send()
        if self.forward:
            for i in range(8):
                self.core_copy(i).wait_send()


def entry_rows(place, offset=(0, 0, 0)):
    bits = [place.low[a][d] for a, d in enumerate(offset)]
    return pl.ds(pl.multiple_of((bits[0] * 2 + bits[1]) * TILE + bits[2] * ROWS, ROWS), ROWS)


GATHER_SEMS = [
    pltpu.SemaphoreType.DMA((3, 7)),
    pltpu.SemaphoreType.DMA((3, 7)),
    pltpu.SemaphoreType.DMA((8,)),
    pltpu.SemaphoreType.DMA((8,)),
]


def low_lanes(rows):
    return lax.broadcasted_iota(jnp.int32, (rows, LANES), 1) < HDIM


def pack_heads(first_ref, second_ref, packed, scale=None):
    low = low_lanes(ROWS)
    for j in range(HEADS // 2):
        columns = slice(j * LANES, (j + 1) * LANES)
        one = first_ref[:, columns].astype(F32)
        two = second_ref[:, columns].astype(F32)
        if scale is not None:
            one = one * scale
        packed[2 * j] = jnp.where(low, one, pltpu.roll(two, HDIM, 1)).astype(BF16)
        packed[2 * j + 1] = jnp.where(low, pltpu.roll(one, HDIM, 1), two).astype(BF16)


def slot_lists(mask, order, place):
    def dot(a, b, dims=NN):
        return lax.dot_general(a.astype(BF16), b.astype(BF16), dims, preferred_element_type=F32)

    def iota(shape, dim):
        return lax.broadcasted_iota(jnp.int32, shape, dim)

    def one_if(condition):
        return jnp.where(condition, 1.0, 0.0).astype(F32)

    slot = iota((32, SLOTS), 1)
    x = 2 * (slot >> 5) + ((slot >> 1) & 1)
    y = 2 * ((slot >> 4) & 1) + (slot & 1)
    from_frame = one_if((x * 4 + y) * 2 + ((slot >> 2) & 1) == iota((32, SLOTS), 0))
    frames = dot(jnp.broadcast_to(order.astype(F32), (8, 32)), from_frame)
    tiles = (2.0 * frames + ((iota((8, SLOTS), 1) >> 3) & 1).astype(F32))[0:1]
    is_tile = one_if(iota((SLOTS, SLOTS), 0).astype(F32) == tiles)
    row = iota((8, SLOTS), 0)
    is_own = one_if(iota((8, SLOTS), 1) == place.block() * TILES + (row & 3))
    own_tiles = dot(is_own, is_tile, NT)
    mask = one_if(mask == 1)
    attends = dot(dot(own_tiles, mask), is_tile)
    attended = dot(dot(own_tiles, mask, NT), is_tile)
    allowed = jnp.where(row < TILES, attends, attended)
    ahead = dot(allowed, one_if(iota((SLOTS, SLOTS), 0) < iota((SLOTS, SLOTS), 1)))
    count = jnp.sum(allowed, axis=1, keepdims=True)
    ahead = jnp.where(allowed > 0.5, ahead, -1.0)
    place_in_list = iota((LANES, SLOTS), 0).astype(F32)
    slots = iota((8, SLOTS), 1).astype(F32)
    lists = jnp.zeros((8, LANES), F32)
    rows, lanes = iota((8, LANES), 0), iota((8, LANES), 1)
    for r in range(8):
        lists = jnp.where(rows == r, dot(slots, one_if(place_in_list == ahead[r : r + 1]), NT), lists)
    lists = jnp.where(lanes.astype(F32) < count, lists, lists[:, 0:1])
    return jnp.where(lanes == LANES - 1, count, lists).astype(jnp.int32)


def enter_kernel(q_ref, k_ref, v_ref, g_ref, mask_ref, order_ref, kv_ref, qg_ref, kv_own, qg_own, list_ref,
                 q_buf, k_buf, v_buf, g_buf, mask_buf, order_buf, kv_pack, qg_pack, load_sems,
                 pair_send, pair_recv, *gather_sems):
    place = Place()
    wait_all = greet(
        [place.pair_device(o) for o in OFFSETS]
        + [place.mirror_device(u) for u in UNIT]
        + [place.mirror_device((0, 0, 0), 1)]
    )
    loads = [
        pltpu.make_async_copy(source, target, load_sems.at[i])
        for i, (source, target) in enumerate([
            (k_ref, k_buf), (v_ref, v_buf), (q_ref, q_buf), (g_ref, g_buf),
            (mask_ref, mask_buf), (order_ref, order_buf),
        ])
    ]
    for load in loads:
        load.start()
    own = place.block()
    packs, landings = (kv_pack, qg_pack), (kv_ref.at[own], qg_ref.at[own])

    def pair_copy(which, i, arriving=False):
        rows = entry_rows(place, OFFSETS[i] if arriving else (0, 0, 0))
        return remote(packs[which].at[place.head(OFFSETS[i])], landings[which].at[rows, :],
                      pair_send.at[which, i], pair_recv.at[which, i], place.pair_device(OFFSETS[i]))

    def hand_out(which):
        for i in range(7):
            pair_copy(which, i).start()
        here_too = packs[which][place.head()]
        landings[which][entry_rows(place), :] = here_too

    def taken_in(which):
        for i in range(7):
            pair_copy(which, i, True).wait_recv()

    gathers = [CubeGather(kv_ref, place, gather_sems[:4]), CubeGather(qg_ref, place, gather_sems[4:])]
    loads[0].wait()
    loads[1].wait()
    pack_heads(k_buf, v_buf, kv_pack)
    wait_all()
    hand_out(0)
    loads[2].wait()
    loads[3].wait()
    pack_heads(q_buf, g_buf, qg_pack, HDIM ** -0.5)
    hand_out(1)
    loads[4].wait()
    loads[5].wait()
    list_ref[...] = slot_lists(mask_buf[...], order_buf[...], place)
    for which in range(2):
        taken_in(which)
        gathers[which].begin()
        (kv_own, qg_own)[which][...] = landings[which][...]
    for k, onward in ((0, (2, 4)), (1, (5,)), (2, (6,)), (3, ()), (4, ()), (5, ()), (6, ())):
        for gather in gathers:
            gather.relay_step(k, onward)
    for which in range(2):
        for i in range(7):
            pair_copy(which, i).wait_send()
    for gather in gathers:
        gather.finish()


def enter(q, k, v, g, tile_mask, frame_order):
    entry = pltpu.VMEM((ROWS, HEADS * HDIM), BF16)
    pack = pltpu.VMEM((HEADS, ROWS, LANES), BF16)
    return pl.pallas_call(
        enter_kernel,
        name="enter",
        out_shape=(
            jax.ShapeDtypeStruct((BLOCKS, BLOCK, LANES), BF16),
            jax.ShapeDtypeStruct((BLOCKS, BLOCK, LANES), BF16),
            jax.ShapeDtypeStruct((BLOCK, LANES), BF16),
            jax.ShapeDtypeStruct((BLOCK, LANES), BF16),
            jax.ShapeDtypeStruct((8, LANES), jnp.int32),
        ),
        in_specs=[HBM_SPEC] * 6,
        out_specs=(VMEM_SPEC,) * 5,
        scratch_shapes=[entry] * 4 + [
            pltpu.VMEM(tile_mask.shape, jnp.int32),
            pltpu.VMEM((1, frame_order.shape[0]), jnp.int32),
            pack,
            pack,
            pltpu.SemaphoreType.DMA((6,)),
            pltpu.SemaphoreType.DMA((2, 7)),
            pltpu.SemaphoreType.DMA((2, 7)),
        ] + GATHER_SEMS + GATHER_SEMS[:2],
        compiler_params=pltpu.CompilerParams(
            collective_id=0, has_side_effects=True, vmem_limit_bytes=16 * 2**20
        ),
    )(*[pltpu.with_memory_space_constraint(a, pltpu.HBM) for a in (q, k, v, g, tile_mask, frame_order.reshape(1, -1))])


def share_kernel(qg_mine, stat_own, dq_ref, qg_ref, stat_ref, dq_got, stat_send, stat_recv, pair_send, pair_recv,
                 core_send, core_recv):
    place = Place()
    peers = [(o, c) for o in OFFSETS for c in (0, 1)] + [((0, 0, 0), 1)]
    wait_all = greet(
        [place.mirror_device(*p) for p in peers] + [place.pair_device(o) for o in OFFSETS]
    )
    own = place.block()
    stat_ref[own] = stat_own[...]
    for offset in ALL_OFFSETS:
        qg_ref[place.block(offset)] = qg_mine[place.block(offset)]

    def core_copy(i, arriving=False):
        block = place.block(ALL_OFFSETS[i], int(arriving))
        return remote(qg_mine.at[block], qg_ref.at[block], core_send.at[i], core_recv.at[i],
                      place.mirror_device((0, 0, 0), 1))

    def stat_copy(i, arriving=False):
        offset, flip = peers[i]
        source = place.block(offset, flip) if arriving else own
        part = stat_ref.at[source]
        return remote(part, part, stat_send.at[i], stat_recv.at[i], place.mirror_device(offset, flip))

    def pair_copy(i, arriving=False):
        landing = dq_got.at[place.head(OFFSETS[i]) if arriving else place.head()]
        return remote(dq_ref.at[place.entry(OFFSETS[i])], landing, pair_send.at[i], pair_recv.at[i],
                      place.pair_device(OFFSETS[i]))

    wait_all()
    for i in range(15):
        stat_copy(i).start()
    for i in range(7):
        pair_copy(i).start()
    for i in range(8):
        core_copy(i).start()
    dq_got[place.head()] = dq_ref[place.entry()]
    for i in range(8):
        core_copy(i, True).wait_recv()
    for i in range(15):
        stat_copy(i, True).wait_recv()
    for i in range(7):
        pair_copy(i, True).wait_recv()
    for i in range(8):
        core_copy(i).wait_send()
    for i in range(15):
        stat_copy(i).wait_send()
    for i in range(7):
        pair_copy(i).wait_send()


def share(qg_mine, stat_own, dq):
    return pl.pallas_call(
        share_kernel,
        name="share",
        out_shape=(
            jax.ShapeDtypeStruct((BLOCKS, BLOCK, LANES), BF16),
            jax.ShapeDtypeStruct((BLOCKS, 8, LANES), F32),
            jax.ShapeDtypeStruct((HEADS, ROWS // 2, LANES), BF16),
        ),
        in_specs=[VMEM_SPEC] * 3,
        out_specs=(VMEM_SPEC,) * 3,
        scratch_shapes=[
            pltpu.SemaphoreType.DMA((15,)),
            pltpu.SemaphoreType.DMA((15,)),
            pltpu.SemaphoreType.DMA((7,)),
            pltpu.SemaphoreType.DMA((7,)),
            pltpu.SemaphoreType.DMA((8,)),
            pltpu.SemaphoreType.DMA((8,)),
        ],
        compiler_params=pltpu.CompilerParams(
            collective_id=1, has_side_effects=True, vmem_limit_bytes=8 * 2**20
        ),
    )(qg_mine, stat_own, dq)


def query_kernel(kv_ref, qg_own, list_ref, stat_ref, dq_ref, term_buf, peak_buf, stat_buf):
    low = low_lanes(TILE)
    lane = lax.broadcasted_iota(jnp.int32, (TILE, LANES), 1)
    zero = jnp.zeros((TILE, LANES), BF16)
    zeros = jnp.zeros((TILE, LANES), F32)

    def some_tiles(first, unused):
        span = range(SPAN)
        tiles = [first * SPAN + i for i in span]
        counts = [list_ref[t, LANES - 1] for t in tiles]
        most = functools.reduce(jnp.maximum, counts)
        steps = (jnp.maximum(most - FIRST, 0) + GROUP - 1) // GROUP
        both = [qg_own[t] for t in tiles]

        def over_list(work, state):
            state = work(0, 0, FIRST, state)
            return lax.fori_loop(
                0, steps, lambda step, state: work(step + 1, FIRST + step * GROUP, GROUP, state), state
            )

        def keys_of(i, begin, group):
            return jnp.concatenate([kv_ref[list_ref[tiles[i], begin + u]] for u in range(group)], axis=0)

        def cut(u):
            return slice(u * TILE, (u + 1) * TILE)

        def term_step(step, begin, group, state):
            after = []
            for i in span:
                before, mass = state[2 * i : 2 * i + 2]
                query = jnp.where(low, both[i], zero)
                scores = lax.dot_general(query, keys_of(i, begin, group), NT, preferred_element_type=F32)
                peak = before
                for u in range(group):
                    peak = jnp.maximum(peak, scores[:, cut(u)])
                mass = mass * jnp.exp(before - peak)
                for u in range(group):
                    less = jnp.where(begin + u < counts[i], 0.0, BIG).astype(F32)
                    term = jnp.exp(scores[:, cut(u)] - (peak + less))
                    term_buf[i, begin + u] = term
                    mass = mass + term
                peak_buf[i, step] = peak
                after += [peak, mass]
            return tuple(after)

        state = over_list(term_step, (jnp.full((TILE, LANES), -BIG, F32), zeros) * SPAN)
        peaks, inverses, log_masses = [], [], []
        for i in span:
            lane_peak, lane_mass = state[2 * i : 2 * i + 2]
            peak = jnp.max(lane_peak, axis=1, keepdims=True)
            mass = jnp.sum(lane_mass * jnp.exp(lane_peak - peak), axis=1, keepdims=True)
            peaks.append(peak)
            inverses.append(1.0 / mass)
            log_masses.append(peak + jnp.log(mass))

        def out_step(step, begin, group, outs):
            after = []
            for i in span:
                factor = jnp.exp(peak_buf[i, step] - peaks[i]) * inverses[i]
                peak_buf[i, step] = factor
                probs = [(term_buf[i, begin + u] * factor).astype(BF16) for u in range(group)]
                after.append(outs[i] + lax.dot_general(
                    jnp.concatenate(probs, axis=1), keys_of(i, begin, group), NN, preferred_element_type=F32
                ))
            return tuple(after)

        outs = over_list(out_step, (zeros,) * SPAN)
        deltas = []
        for i in span:
            out = outs[i].astype(BF16).astype(F32)
            deltas.append(jnp.sum(jnp.where(low, 0.0, both[i].astype(F32) * out), axis=1, keepdims=True))

        def grad_step(step, begin, group, accs):
            after = []
            for i in span:
                keys = keys_of(i, begin, group)
                factor = peak_buf[i, step]
                grad = jnp.where(low, zero, both[i])
                prob_grad = lax.dot_general(grad, keys, NT, preferred_element_type=F32)
                score_grad = [
                    ((term_buf[i, begin + u] * factor) * (prob_grad[:, cut(u)] - deltas[i])).astype(BF16)
                    for u in range(group)
                ]
                after.append(accs[i] + lax.dot_general(
                    jnp.concatenate(score_grad, axis=1), keys, NN, preferred_element_type=F32
                ))
            return tuple(after)

        accs = over_list(grad_step, (zeros,) * SPAN)
        low_part = low_lanes(ROWS // 2)
        stats = stat_buf[...]
        for i in span:
            acc = accs[i] * HDIM ** -0.5
            for j in range(2):
                top = acc[j * ROWS : j * ROWS + ROWS // 2]
                bottom = acc[j * ROWS + ROWS // 2 : (j + 1) * ROWS]
                dq_ref[2 * tiles[i] + j] = jnp.where(low_part, top, pltpu.roll(bottom, HDIM, 1)).astype(BF16)
            stats = jnp.where(lane == tiles[i], log_masses[i], stats)
            stats = jnp.where(lane == TILES + tiles[i], deltas[i], stats)
        stat_buf[...] = stats
        return unused

    stat_buf[...] = zeros
    lax.fori_loop(0, TILES // SPAN, some_tiles, 0)
    stat_ref[...] = stat_buf[...].T[:8]


def query_side(kv, qg_own, lists):
    return pl.pallas_call(
        query_kernel,
        name="query_side",
        out_shape=(
            jax.ShapeDtypeStruct((8, LANES), F32),
            jax.ShapeDtypeStruct((2 * TILES, ROWS // 2, LANES), BF16),
        ),
        in_specs=[VMEM_SPEC, VMEM_SPEC, SMEM_SPEC],
        out_specs=(VMEM_SPEC,) * 2,
        scratch_shapes=[
            pltpu.VMEM((SPAN, SLOTS + GROUP, TILE, TILE), F32),
            pltpu.VMEM((SPAN, SLOTS // GROUP, TILE, LANES), F32),
            pltpu.VMEM((TILE, LANES), F32),
        ],
        compiler_params=pltpu.CompilerParams(vmem_limit_bytes=34 * 2**20),
    )(kv.reshape(SLOTS, TILE, LANES), qg_own.reshape(TILES, TILE, LANES), lists)


def key_kernel(qg_ref, stat_ref, kv_own, list_ref, dkv_ref, rows_ref):
    for b in range(BLOCKS):
        for t in range(TILES):
            rows_ref[b * TILES + t, 0:1, :] = stat_ref[b, t : t + 1, :]
            rows_ref[b * TILES + t, 1:2, :] = stat_ref[b, TILES + t : TILES + t + 1, :]
    low = low_lanes(TILE)
    zero = jnp.zeros((TILE, LANES), BF16)

    def some_tiles(first, unused):
        span = range(KEY_SPAN)
        tiles = [first * KEY_SPAN + i for i in span]
        counts = [list_ref[TILES + t, LANES - 1] for t in tiles]
        most = functools.reduce(jnp.maximum, counts)
        steps = (most + KEY_GROUP - 1) // KEY_GROUP
        stacks = [
            jnp.concatenate([jnp.where(low, kv_own[t], zero), jnp.where(low, zero, kv_own[t])], axis=0)
            for t in tiles
        ]

        def step_terms(step, accs):
            after = []
            for i in span:
                lefts, rights = [], []
                for u in range(KEY_GROUP):
                    slot = list_ref[TILES + tiles[i], step * KEY_GROUP + u]
                    less = jnp.where(step * KEY_GROUP + u < counts[i], 0.0, BIG).astype(F32)
                    queries = qg_ref[slot]
                    products = lax.dot_general(stacks[i], queries, NT, preferred_element_type=F32)
                    probs = jnp.exp(products[:TILE] - (rows_ref[slot, 0:1, :] + less))
                    score_grad = probs * (products[TILE:] - rows_ref[slot, 1:2, :])
                    lefts += [score_grad.astype(BF16), probs.astype(BF16)]
                    rights += [jnp.where(low, queries, zero), jnp.where(low, zero, queries)]
                after.append(accs[i] + lax.dot_general(
                    jnp.concatenate(lefts, axis=1), jnp.concatenate(rights, axis=0), NN,
                    preferred_element_type=F32,
                ))
            return tuple(after)

        accs = lax.fori_loop(0, steps, step_terms, (jnp.zeros((TILE, LANES), F32),) * KEY_SPAN)
        for i in span:
            dkv_ref[tiles[i]] = accs[i].astype(BF16)
        return unused

    lax.fori_loop(0, TILES // KEY_SPAN, some_tiles, 0)


def key_side(qg, stats, kv_own, lists):
    return pl.pallas_call(
        key_kernel,
        name="key_side",
        out_shape=jax.ShapeDtypeStruct((TILES, TILE, LANES), BF16),
        in_specs=[VMEM_SPEC, VMEM_SPEC, VMEM_SPEC, SMEM_SPEC],
        out_specs=VMEM_SPEC,
        scratch_shapes=[
            pltpu.VMEM((SLOTS, 8, LANES), F32),
        ],
        compiler_params=pltpu.CompilerParams(vmem_limit_bytes=34 * 2**20),
    )(qg.reshape(SLOTS, TILE, LANES), stats, kv_own.reshape(TILES, TILE, LANES), lists)


def leave_kernel(dkv_ref, dkv_got, pair_send, pair_recv):
    place = Place()
    wait_all = greet([place.pair_device(o) for o in OFFSETS])

    def pair_copy(i, arriving=False):
        landing = dkv_got.at[place.head(OFFSETS[i]) if arriving else place.head()]
        return remote(dkv_ref.at[place.entry(OFFSETS[i])], landing, pair_send.at[i], pair_recv.at[i],
                      place.pair_device(OFFSETS[i]))

    wait_all()
    for i in range(7):
        pair_copy(i).start()
    dkv_got[place.head()] = dkv_ref[place.entry()]
    for i in range(7):
        pair_copy(i, True).wait_recv()
    for i in range(7):
        pair_copy(i).wait_send()


def unpack_kernel(dq_got, dkv_got, q_ref, k_ref, v_ref, q_out, k_out, v_out, sems):
    def halves(got, j):
        one, two = got[2 * j].astype(F32), got[2 * j + 1].astype(F32)
        low = low_lanes(one.shape[0])
        return (
            jnp.where(low, one, pltpu.roll(two, HDIM, 1)).astype(BF16),
            jnp.where(low, pltpu.roll(one, HDIM, 1), two).astype(BF16),
        )

    for j in range(HEADS // 2):
        columns = slice(j * LANES, (j + 1) * LANES)
        k_out[:, columns], v_out[:, columns] = halves(dkv_got, j)
        q_out[0 : ROWS // 2, columns], q_out[ROWS // 2 : ROWS, columns] = halves(dq_got, j)
    copies = [
        pltpu.make_async_copy(source, target, sems.at[i])
        for i, (source, target) in enumerate([(q_out, q_ref), (k_out, k_ref), (v_out, v_ref)])
    ]
    for copy in copies:
        copy.start()
    for copy in copies:
        copy.wait()


def leave(dq_got, dkv):
    dkv_got = pl.pallas_call(
        leave_kernel,
        name="leave",
        out_shape=jax.ShapeDtypeStruct((HEADS, ROWS, LANES), BF16),
        in_specs=[VMEM_SPEC],
        out_specs=VMEM_SPEC,
        scratch_shapes=[pltpu.SemaphoreType.DMA((7,)), pltpu.SemaphoreType.DMA((7,))],
        compiler_params=pltpu.CompilerParams(
            collective_id=2, has_side_effects=True, vmem_limit_bytes=8 * 2**20
        ),
    )(dkv.reshape(HEADS, ROWS, LANES))
    shape = (ROWS, HEADS * HDIM)
    return pl.pallas_call(
        unpack_kernel,
        name="unpack",
        out_shape=(jax.ShapeDtypeStruct(shape, BF16),) * 3,
        in_specs=[VMEM_SPEC] * 2,
        out_specs=(HBM_SPEC,) * 3,
        scratch_shapes=[pltpu.VMEM(shape, BF16)] * 3 + [pltpu.SemaphoreType.DMA((3,))],
        compiler_params=pltpu.CompilerParams(vmem_limit_bytes=8 * 2**20),
    )(dq_got, dkv_got)


def body(queries, keys, values, out_grad, tile_mask, frame_order):
    kv, qg_mine, kv_own, qg_own, lists = enter(queries, keys, values, out_grad, tile_mask, frame_order)
    stats_own, dq = query_side(kv, qg_own, lists)
    qg, stats, dq_got = share(qg_mine, stats_own, dq)
    return leave(dq_got, key_side(qg, stats, kv_own, lists))


def solution(mesh):
    whole = P(("blk", "head"), None)
    return jax.shard_map(
        body,
        mesh=mesh,
        in_specs=(whole,) * 4 + (P(), P()),
        out_specs=(whole,) * 3,
        check_vma=False,
    )
```

```python
import functools

import jax
import jax.numpy as jnp
from jax import lax
from jax.experimental import pallas as pl
from jax.experimental.pallas import tpu as pltpu
from jax.sharding import PartitionSpec as P

HDIM = 64
TILE = 128
LANES = 128
HEADS = 8
ROWS = 64
TILES = 4
BLOCK = TILES * TILE
BLOCKS = 16
SLOTS = BLOCKS * TILES
FIRST = 24
GROUP = 8
KEY_GROUP = 8
SPAN = 4
KEY_SPAN = 4
PIECES = ((0, 176), (176, 176), (352, 160))
MESH = pl.DeviceIdType.MESH
F32 = jnp.float32
BF16 = jnp.bfloat16
BIG = 1e30
NT = (((1,), (1,)), ((), ()))
NN = (((1,), (0,)), ((), ()))
HBM_SPEC = pl.BlockSpec(memory_space=pltpu.HBM)
VMEM_SPEC = pl.BlockSpec(memory_space=pltpu.VMEM)
SMEM_SPEC = pl.BlockSpec(memory_space=pltpu.SMEM)


class Place:
    def __init__(self):
        blk = lax.axis_index("blk")
        z = lax.axis_index("head")
        x = blk // 8
        rest = blk - 8 * x
        y = rest // 2
        self.core = rest - 2 * y
        self.other = 1 - self.core
        self.at = (x, y, z)
        self.high = [(h, 1 - h) for h in (v // 2 for v in self.at)]
        self.low = [(l, 1 - l) for l in (v - 2 * h[0] for v, h in zip(self.at, self.high))]
        halves = [h[0] + l[0] - 2 * h[0] * l[0] for h, l in zip(self.high, self.low)]
        self.half = [(h, 1 - h) for h in halves]
        self.pair = [(v, v + 1 - 2 * l[0]) for v, l in zip(self.at, self.low)]
        self.mirror = [(v, 3 - v) for v in self.at]
        self.known = {}

    def once(self, key, work):
        if key not in self.known:
            self.known[key] = work()
        return self.known[key]

    def device(self, table, offset, flip):
        x, y, z = [t[d] for t, d in zip(table, offset)]
        return ((x * 4 + y) * 2 + (self.other if flip else self.core), z)

    def pair_device(self, offset):
        return self.once(("pair", offset), lambda: self.device(self.pair, offset, 0))

    def mirror_device(self, offset, flip=0):
        return self.once(("mirror", offset, flip), lambda: self.device(self.mirror, offset, flip))

    def number(self, bits, offset):
        return (bits[0][offset[0]] * 2 + bits[1][offset[1]]) * 2 + bits[2][offset[2]]

    def head(self, offset=(0, 0, 0)):
        return self.once(("head", offset), lambda: self.number(self.half, offset))

    def entry(self, offset=(0, 0, 0)):
        return self.once(("entry", offset), lambda: self.number(self.low, offset))

    def block(self, offset=(0, 0, 0), flip=0):
        return self.once(
            ("block", offset, flip),
            lambda: self.number(self.high, offset) * 2 + (self.other if flip else self.core),
        )


ALL_OFFSETS = [(a, b, c) for a in (0, 1) for b in (0, 1) for c in (0, 1)]
OFFSETS = sorted(ALL_OFFSETS[1:], key=sum, reverse=True)


def remote(src, dst, send, recv, target):
    return pltpu.make_async_remote_copy(
        src_ref=src, dst_ref=dst, send_sem=send, recv_sem=recv, device_id=target, device_id_type=MESH
    )


def greet(targets):
    barrier = pltpu.get_barrier_semaphore()
    for target in targets:
        pl.semaphore_signal(barrier, inc=1, device_id=target, device_id_type=MESH)
    return lambda: pl.semaphore_wait(barrier, len(targets))


UNIT = [(1, 0, 0), (0, 1, 0), (0, 0, 1)]


def plus(*offsets):
    return tuple(sum(v) for v in zip(*offsets))


class CubeGather:
    def __init__(self, ref, place, sems):
        self.ref, self.place = ref, place
        self.forward = len(sems) == 4
        self.send, self.recv = sems[:2]
        if self.forward:
            self.core_send, self.core_recv = sems[2:]
        self.pieces = [0] * len(ALL_OFFSETS)

    def hops(self, piece):
        a1, a2, a3 = [(piece + i) % 3 for i in range(3)]
        u1, u2, o = UNIT[a1], UNIT[a2], (0, 0, 0)
        return [(a1, o), (a2, o), (a2, u1), (a3, o), (a3, u1), (a3, u2), (a3, plus(u1, u2))]

    def hop_copy(self, piece, k, arriving=False):
        axis, offset = self.hops(piece)[k]
        if arriving:
            offset = plus(offset, UNIT[axis])
        first, count = PIECES[piece]
        part = self.ref.at[self.place.block(offset), pl.ds(first, count), :]
        return remote(part, part, self.send.at[piece, k], self.recv.at[piece, k],
                      self.place.mirror_device(UNIT[axis]))

    def core_copy(self, i, arriving=False):
        part = self.ref.at[self.place.block(ALL_OFFSETS[i], int(arriving))]
        return remote(part, part, self.core_send.at[i], self.core_recv.at[i],
                      self.place.mirror_device((0, 0, 0), 1))

    def begin(self):
        for k in (0, 1, 3):
            for p in range(3):
                self.hop_copy(p, k).start()
        if self.forward:
            self.core_copy(0).start()

    def relay_step(self, k, onward):
        for p in range(3):
            self.hop_copy(p, k, True).wait_recv()
            for j in onward:
                self.hop_copy(p, j).start()
            axis, offset = self.hops(p)[k]
            i = ALL_OFFSETS.index(plus(offset, UNIT[axis]))
            self.pieces[i] += 1
            if self.forward and self.pieces[i] == 3:
                self.core_copy(i).start()

    def finish(self):
        if self.forward:
            for i in range(8):
                self.core_copy(i, True).wait_recv()
        for p in range(3):
            for k in range(7):
                self.hop_copy(p, k).wait_send()
        if self.forward:
            for i in range(8):
                self.core_copy(i).wait_send()


def entry_rows(place, offset=(0, 0, 0)):
    bits = [place.low[a][d] for a, d in enumerate(offset)]
    return pl.ds(pl.multiple_of((bits[0] * 2 + bits[1]) * TILE + bits[2] * ROWS, ROWS), ROWS)


GATHER_SEMS = [
    pltpu.SemaphoreType.DMA((3, 7)),
    pltpu.SemaphoreType.DMA((3, 7)),
    pltpu.SemaphoreType.DMA((8,)),
    pltpu.SemaphoreType.DMA((8,)),
]


def low_lanes(rows):
    return lax.broadcasted_iota(jnp.int32, (rows, LANES), 1) < HDIM


def pack_heads(first_ref, second_ref, packed, scale=None):
    low = low_lanes(ROWS)
    for j in range(HEADS // 2):
        columns = slice(j * LANES, (j + 1) * LANES)
        one = first_ref[:, columns].astype(F32)
        two = second_ref[:, columns].astype(F32)
        if scale is not None:
            one = one * scale
        packed[2 * j] = jnp.where(low, one, pltpu.roll(two, HDIM, 1)).astype(BF16)
        packed[2 * j + 1] = jnp.where(low, pltpu.roll(one, HDIM, 1), two).astype(BF16)


def slot_lists(mask, order, place):
    def dot(a, b, dims=NN):
        return lax.dot_general(a.astype(BF16), b.astype(BF16), dims, preferred_element_type=F32)

    def iota(shape, dim):
        return lax.broadcasted_iota(jnp.int32, shape, dim)

    def one_if(condition):
        return jnp.where(condition, 1.0, 0.0).astype(F32)

    slot = iota((32, SLOTS), 1)
    x = 2 * (slot >> 5) + ((slot >> 1) & 1)
    y = 2 * ((slot >> 4) & 1) + (slot & 1)
    from_frame = one_if((x * 4 + y) * 2 + ((slot >> 2) & 1) == iota((32, SLOTS), 0))
    frames = dot(jnp.broadcast_to(order.astype(F32), (8, 32)), from_frame)
    tiles = (2.0 * frames + ((iota((8, SLOTS), 1) >> 3) & 1).astype(F32))[0:1]
    is_tile = one_if(iota((SLOTS, SLOTS), 0).astype(F32) == tiles)
    row = iota((8, SLOTS), 0)
    is_own = one_if(iota((8, SLOTS), 1) == place.block() * TILES + (row & 3))
    own_tiles = dot(is_own, is_tile, NT)
    mask = one_if(mask == 1)
    attends = dot(dot(own_tiles, mask), is_tile)
    attended = dot(dot(own_tiles, mask, NT), is_tile)
    allowed = jnp.where(row < TILES, attends, attended)
    ahead = dot(allowed, one_if(iota((SLOTS, SLOTS), 0) < iota((SLOTS, SLOTS), 1)))
    count = jnp.sum(allowed, axis=1, keepdims=True)
    ahead = jnp.where(allowed > 0.5, ahead, -1.0)
    place_in_list = iota((LANES, SLOTS), 0).astype(F32)
    slots = iota((8, SLOTS), 1).astype(F32)
    lists = jnp.zeros((8, LANES), F32)
    rows, lanes = iota((8, LANES), 0), iota((8, LANES), 1)
    for r in range(8):
        lists = jnp.where(rows == r, dot(slots, one_if(place_in_list == ahead[r : r + 1]), NT), lists)
    lists = jnp.where(lanes.astype(F32) < count, lists, lists[:, 0:1])
    return jnp.where(lanes == LANES - 1, count, lists).astype(jnp.int32)


def enter_kernel(q_ref, k_ref, v_ref, g_ref, mask_ref, order_ref, kv_ref, qg_ref, kv_own, qg_own, list_ref,
                 q_buf, k_buf, v_buf, g_buf, mask_buf, order_buf, kv_pack, qg_pack, load_sems,
                 pair_send, pair_recv, *gather_sems):
    place = Place()
    wait_all = greet(
        [place.pair_device(o) for o in OFFSETS]
        + [place.mirror_device(u) for u in UNIT]
        + [place.mirror_device((0, 0, 0), 1)]
    )
    loads = [
        pltpu.make_async_copy(source, target, load_sems.at[i])
        for i, (source, target) in enumerate([
            (k_ref, k_buf), (v_ref, v_buf), (q_ref, q_buf), (g_ref, g_buf),
            (mask_ref, mask_buf), (order_ref, order_buf),
        ])
    ]
    for load in loads:
        load.start()
    own = place.block()
    packs, landings = (kv_pack, qg_pack), (kv_ref.at[own], qg_ref.at[own])

    def pair_copy(which, i, arriving=False):
        rows = entry_rows(place, OFFSETS[i] if arriving else (0, 0, 0))
        return remote(packs[which].at[place.head(OFFSETS[i])], landings[which].at[rows, :],
                      pair_send.at[which, i], pair_recv.at[which, i], place.pair_device(OFFSETS[i]))

    def hand_out(which):
        for i in range(7):
            pair_copy(which, i).start()
        here_too = packs[which][place.head()]
        landings[which][entry_rows(place), :] = here_too

    def taken_in(which):
        for i in range(7):
            pair_copy(which, i, True).wait_recv()

    gathers = [CubeGather(kv_ref, place, gather_sems[:4]), CubeGather(qg_ref, place, gather_sems[4:])]
    loads[0].wait()
    loads[1].wait()
    pack_heads(k_buf, v_buf, kv_pack)
    wait_all()
    hand_out(0)
    loads[2].wait()
    loads[3].wait()
    pack_heads(q_buf, g_buf, qg_pack, HDIM ** -0.5)
    hand_out(1)
    loads[4].wait()
    loads[5].wait()
    list_ref[...] = slot_lists(mask_buf[...], order_buf[...], place)
    for which in range(2):
        taken_in(which)
        gathers[which].begin()
        (kv_own, qg_own)[which][...] = landings[which][...]
    gathers[0].relay_step(0, (2, 4))
    gathers[1].relay_step(0, (2, 4))
    gathers[0].relay_step(1, (5,))
    gathers[1].relay_step(1, (5,))
    gathers[0].relay_step(2, (6,))
    gathers[1].relay_step(2, (6,))
    gathers[0].relay_step(3, ())
    gathers[0].relay_step(4, ())
    gathers[0].relay_step(5, ())
    gathers[0].relay_step(6, ())
    gathers[1].relay_step(3, ())
    gathers[1].relay_step(4, ())
    gathers[1].relay_step(5, ())
    gathers[1].relay_step(6, ())
    for which in range(2):
        for i in range(7):
            pair_copy(which, i).wait_send()
    for gather in gathers:
        gather.finish()


def enter(q, k, v, g, tile_mask, frame_order):
    entry = pltpu.VMEM((ROWS, HEADS * HDIM), BF16)
    pack = pltpu.VMEM((HEADS, ROWS, LANES), BF16)
    return pl.pallas_call(
        enter_kernel,
        name="enter",
        out_shape=(
            jax.ShapeDtypeStruct((BLOCKS, BLOCK, LANES), BF16),
            jax.ShapeDtypeStruct((BLOCKS, BLOCK, LANES), BF16),
            jax.ShapeDtypeStruct((BLOCK, LANES), BF16),
            jax.ShapeDtypeStruct((BLOCK, LANES), BF16),
            jax.ShapeDtypeStruct((8, LANES), jnp.int32),
        ),
        in_specs=[HBM_SPEC] * 6,
        out_specs=(VMEM_SPEC,) * 5,
        scratch_shapes=[entry] * 4 + [
            pltpu.VMEM(tile_mask.shape, jnp.int32),
            pltpu.VMEM((1, frame_order.shape[0]), jnp.int32),
            pack,
            pack,
            pltpu.SemaphoreType.DMA((6,)),
            pltpu.SemaphoreType.DMA((2, 7)),
            pltpu.SemaphoreType.DMA((2, 7)),
        ] + GATHER_SEMS + GATHER_SEMS[:2],
        compiler_params=pltpu.CompilerParams(
            collective_id=0, has_side_effects=True, vmem_limit_bytes=16 * 2**20
        ),
    )(*[pltpu.with_memory_space_constraint(a, pltpu.HBM) for a in (q, k, v, g, tile_mask, frame_order.reshape(1, -1))])


def share_kernel(qg_mine, stat_own, dq_ref, qg_ref, stat_ref, dq_got, stat_send, stat_recv, pair_send, pair_recv,
                 core_send, core_recv):
    place = Place()
    peers = [(o, c) for o in OFFSETS for c in (0, 1)] + [((0, 0, 0), 1)]
    wait_all = greet(
        [place.mirror_device(*p) for p in peers] + [place.pair_device(o) for o in OFFSETS]
    )
    own = place.block()
    stat_ref[own] = stat_own[...]
    for offset in ALL_OFFSETS:
        qg_ref[place.block(offset)] = qg_mine[place.block(offset)]

    def core_copy(i, arriving=False):
        block = place.block(ALL_OFFSETS[i], int(arriving))
        return remote(qg_mine.at[block], qg_ref.at[block], core_send.at[i], core_recv.at[i],
                      place.mirror_device((0, 0, 0), 1))

    def stat_copy(i, arriving=False):
        offset, flip = peers[i]
        source = place.block(offset, flip) if arriving else own
        part = stat_ref.at[source]
        return remote(part, part, stat_send.at[i], stat_recv.at[i], place.mirror_device(offset, flip))

    def pair_copy(i, arriving=False):
        landing = dq_got.at[place.head(OFFSETS[i]) if arriving else place.head()]
        return remote(dq_ref.at[place.entry(OFFSETS[i])], landing, pair_send.at[i], pair_recv.at[i],
                      place.pair_device(OFFSETS[i]))

    wait_all()
    for i in range(15):
        stat_copy(i).start()
    for i in range(8):
        core_copy(i).start()
    for i in range(7):
        pair_copy(i).start()
    dq_got[place.head()] = dq_ref[place.entry()]
    for i in range(8):
        core_copy(i, True).wait_recv()
    for i in range(15):
        stat_copy(i, True).wait_recv()
    for i in range(7):
        pair_copy(i, True).wait_recv()
    for i in range(8):
        core_copy(i).wait_send()
    for i in range(15):
        stat_copy(i).wait_send()
    for i in range(7):
        pair_copy(i).wait_send()


def share(qg_mine, stat_own, dq):
    return pl.pallas_call(
        share_kernel,
        name="share",
        out_shape=(
            jax.ShapeDtypeStruct((BLOCKS, BLOCK, LANES), BF16),
            jax.ShapeDtypeStruct((BLOCKS, 8, LANES), F32),
            jax.ShapeDtypeStruct((HEADS, ROWS // 2, LANES), BF16),
        ),
        in_specs=[VMEM_SPEC] * 3,
        out_specs=(VMEM_SPEC,) * 3,
        scratch_shapes=[
            pltpu.SemaphoreType.DMA((15,)),
            pltpu.SemaphoreType.DMA((15,)),
            pltpu.SemaphoreType.DMA((7,)),
            pltpu.SemaphoreType.DMA((7,)),
            pltpu.SemaphoreType.DMA((8,)),
            pltpu.SemaphoreType.DMA((8,)),
        ],
        compiler_params=pltpu.CompilerParams(
            collective_id=1, has_side_effects=True, vmem_limit_bytes=8 * 2**20
        ),
    )(qg_mine, stat_own, dq)


def query_kernel(kv_ref, qg_own, list_ref, stat_ref, dq_ref, term_buf, peak_buf, stat_buf):
    low = low_lanes(TILE)
    lane = lax.broadcasted_iota(jnp.int32, (TILE, LANES), 1)
    zero = jnp.zeros((TILE, LANES), BF16)
    zeros = jnp.zeros((TILE, LANES), F32)

    def some_tiles(first, unused):
        span = range(SPAN)
        tiles = [first * SPAN + i for i in span]
        counts = [list_ref[t, LANES - 1] for t in tiles]
        most = functools.reduce(jnp.maximum, counts)
        steps = (jnp.maximum(most - FIRST, 0) + GROUP - 1) // GROUP
        both = [qg_own[t] for t in tiles]

        def over_list(work, state):
            state = work(0, 0, FIRST, state)
            return lax.fori_loop(
                0, steps, lambda step, state: work(step + 1, FIRST + step * GROUP, GROUP, state), state
            )

        def keys_of(i, begin, group):
            return jnp.concatenate([kv_ref[list_ref[tiles[i], begin + u]] for u in range(group)], axis=0)

        def cut(u):
            return slice(u * TILE, (u + 1) * TILE)

        def term_step(step, begin, group, state):
            after = []
            for i in span:
                before, mass = state[2 * i : 2 * i + 2]
                query = jnp.where(low, both[i], zero)
                scores = lax.dot_general(query, keys_of(i, begin, group), NT, preferred_element_type=F32)
                peak = before
                for u in range(group):
                    peak = jnp.maximum(peak, scores[:, cut(u)])
                mass = mass * jnp.exp(before - peak)
                for u in range(group):
                    less = jnp.where(begin + u < counts[i], 0.0, BIG).astype(F32)
                    term = jnp.exp(scores[:, cut(u)] - (peak + less))
                    term_buf[i, begin + u] = term
                    mass = mass + term
                peak_buf[i, step] = peak
                after += [peak, mass]
            return tuple(after)

        state = over_list(term_step, (jnp.full((TILE, LANES), -BIG, F32), zeros) * SPAN)
        peaks, inverses, log_masses = [], [], []
        for i in span:
            lane_peak, lane_mass = state[2 * i : 2 * i + 2]
            peak = jnp.max(lane_peak, axis=1, keepdims=True)
            mass = jnp.sum(lane_mass * jnp.exp(lane_peak - peak), axis=1, keepdims=True)
            peaks.append(peak)
            inverses.append(1.0 / mass)
            log_masses.append(peak + jnp.log(mass))

        def out_step(step, begin, group, outs):
            after = []
            for i in span:
                factor = jnp.exp(peak_buf[i, step] - peaks[i]) * inverses[i]
                peak_buf[i, step] = factor
                probs = [(term_buf[i, begin + u] * factor).astype(BF16) for u in range(group)]
                after.append(outs[i] + lax.dot_general(
                    jnp.concatenate(probs, axis=1), keys_of(i, begin, group), NN, preferred_element_type=F32
                ))
            return tuple(after)

        outs = over_list(out_step, (zeros,) * SPAN)
        deltas = []
        for i in span:
            out = outs[i].astype(BF16).astype(F32)
            deltas.append(jnp.sum(jnp.where(low, 0.0, both[i].astype(F32) * out), axis=1, keepdims=True))

        def grad_step(step, begin, group, accs):
            after = []
            for i in span:
                keys = keys_of(i, begin, group)
                factor = peak_buf[i, step]
                grad = jnp.where(low, zero, both[i])
                prob_grad = lax.dot_general(grad, keys, NT, preferred_element_type=F32)
                score_grad = [
                    ((term_buf[i, begin + u] * factor) * (prob_grad[:, cut(u)] - deltas[i])).astype(BF16)
                    for u in range(group)
                ]
                after.append(accs[i] + lax.dot_general(
                    jnp.concatenate(score_grad, axis=1), keys, NN, preferred_element_type=F32
                ))
            return tuple(after)

        accs = over_list(grad_step, (zeros,) * SPAN)
        low_part = low_lanes(ROWS // 2)
        stats = stat_buf[...]
        for i in span:
            acc = accs[i] * HDIM ** -0.5
            for j in range(2):
                top = acc[j * ROWS : j * ROWS + ROWS // 2]
                bottom = acc[j * ROWS + ROWS // 2 : (j + 1) * ROWS]
                dq_ref[2 * tiles[i] + j] = jnp.where(low_part, top, pltpu.roll(bottom, HDIM, 1)).astype(BF16)
            stats = jnp.where(lane == tiles[i], log_masses[i], stats)
            stats = jnp.where(lane == TILES + tiles[i], deltas[i], stats)
        stat_buf[...] = stats
        return unused

    stat_buf[...] = zeros
    lax.fori_loop(0, TILES // SPAN, some_tiles, 0)
    stat_ref[...] = stat_buf[...].T[:8]


def query_side(kv, qg_own, lists):
    return pl.pallas_call(
        query_kernel,
        name="query_side",
        out_shape=(
            jax.ShapeDtypeStruct((8, LANES), F32),
            jax.ShapeDtypeStruct((2 * TILES, ROWS // 2, LANES), BF16),
        ),
        in_specs=[VMEM_SPEC, VMEM_SPEC, SMEM_SPEC],
        out_specs=(VMEM_SPEC,) * 2,
        scratch_shapes=[
            pltpu.VMEM((SPAN, SLOTS + GROUP, TILE, TILE), F32),
            pltpu.VMEM((SPAN, SLOTS // GROUP, TILE, LANES), F32),
            pltpu.VMEM((TILE, LANES), F32),
        ],
        compiler_params=pltpu.CompilerParams(vmem_limit_bytes=34 * 2**20),
    )(kv.reshape(SLOTS, TILE, LANES), qg_own.reshape(TILES, TILE, LANES), lists)


def key_kernel(qg_ref, stat_ref, kv_own, list_ref, dkv_ref, rows_ref):
    for b in range(BLOCKS):
        for t in range(TILES):
            rows_ref[b * TILES + t, 0:1, :] = stat_ref[b, t : t + 1, :]
            rows_ref[b * TILES + t, 1:2, :] = stat_ref[b, TILES + t : TILES + t + 1, :]
    low = low_lanes(TILE)
    zero = jnp.zeros((TILE, LANES), BF16)

    def some_tiles(first, unused):
        span = range(KEY_SPAN)
        tiles = [first * KEY_SPAN + i for i in span]
        counts = [list_ref[TILES + t, LANES - 1] for t in tiles]
        most = functools.reduce(jnp.maximum, counts)
        steps = (most + KEY_GROUP - 1) // KEY_GROUP
        stacks = [
            jnp.concatenate([jnp.where(low, kv_own[t], zero), jnp.where(low, zero, kv_own[t])], axis=0)
            for t in tiles
        ]

        def step_terms(step, accs):
            after = []
            for i in span:
                lefts, rights = [], []
                for u in range(KEY_GROUP):
                    slot = list_ref[TILES + tiles[i], step * KEY_GROUP + u]
                    less = jnp.where(step * KEY_GROUP + u < counts[i], 0.0, BIG).astype(F32)
                    queries = qg_ref[slot]
                    products = lax.dot_general(stacks[i], queries, NT, preferred_element_type=F32)
                    probs = jnp.exp(products[:TILE] - (rows_ref[slot, 0:1, :] + less))
                    score_grad = probs * (products[TILE:] - rows_ref[slot, 1:2, :])
                    lefts += [score_grad.astype(BF16), probs.astype(BF16)]
                    rights += [jnp.where(low, queries, zero), jnp.where(low, zero, queries)]
                after.append(accs[i] + lax.dot_general(
                    jnp.concatenate(lefts, axis=1), jnp.concatenate(rights, axis=0), NN,
                    preferred_element_type=F32,
                ))
            return tuple(after)

        accs = lax.fori_loop(0, steps, step_terms, (jnp.zeros((TILE, LANES), F32),) * KEY_SPAN)
        for i in span:
            dkv_ref[tiles[i]] = accs[i].astype(BF16)
        return unused

    lax.fori_loop(0, TILES // KEY_SPAN, some_tiles, 0)


def key_side(qg, stats, kv_own, lists):
    return pl.pallas_call(
        key_kernel,
        name="key_side",
        out_shape=jax.ShapeDtypeStruct((TILES, TILE, LANES), BF16),
        in_specs=[VMEM_SPEC, VMEM_SPEC, VMEM_SPEC, SMEM_SPEC],
        out_specs=VMEM_SPEC,
        scratch_shapes=[
            pltpu.VMEM((SLOTS, 8, LANES), F32),
        ],
        compiler_params=pltpu.CompilerParams(vmem_limit_bytes=34 * 2**20),
    )(qg.reshape(SLOTS, TILE, LANES), stats, kv_own.reshape(TILES, TILE, LANES), lists)


def leave_kernel(dkv_ref, dkv_got, pair_send, pair_recv):
    place = Place()
    wait_all = greet([place.pair_device(o) for o in OFFSETS])

    def pair_copy(i, arriving=False):
        landing = dkv_got.at[place.head(OFFSETS[i]) if arriving else place.head()]
        return remote(dkv_ref.at[place.entry(OFFSETS[i])], landing, pair_send.at[i], pair_recv.at[i],
                      place.pair_device(OFFSETS[i]))

    wait_all()
    for i in range(7):
        pair_copy(i).start()
    dkv_got[place.head()] = dkv_ref[place.entry()]
    for i in range(7):
        pair_copy(i, True).wait_recv()
    for i in range(7):
        pair_copy(i).wait_send()


def unpack_kernel(dq_got, dkv_got, q_ref, k_ref, v_ref, q_out, k_out, v_out, sems):
    def halves(got, j):
        one, two = got[2 * j].astype(F32), got[2 * j + 1].astype(F32)
        low = low_lanes(one.shape[0])
        return (
            jnp.where(low, one, pltpu.roll(two, HDIM, 1)).astype(BF16),
            jnp.where(low, pltpu.roll(one, HDIM, 1), two).astype(BF16),
        )

    for j in range(HEADS // 2):
        columns = slice(j * LANES, (j + 1) * LANES)
        k_out[:, columns], v_out[:, columns] = halves(dkv_got, j)
        q_out[0 : ROWS // 2, columns], q_out[ROWS // 2 : ROWS, columns] = halves(dq_got, j)
    copies = [
        pltpu.make_async_copy(source, target, sems.at[i])
        for i, (source, target) in enumerate([(q_out, q_ref), (k_out, k_ref), (v_out, v_ref)])
    ]
    for copy in copies:
        copy.start()
    for copy in copies:
        copy.wait()


def leave(dq_got, dkv):
    dkv_got = pl.pallas_call(
        leave_kernel,
        name="leave",
        out_shape=jax.ShapeDtypeStruct((HEADS, ROWS, LANES), BF16),
        in_specs=[VMEM_SPEC],
        out_specs=VMEM_SPEC,
        scratch_shapes=[pltpu.SemaphoreType.DMA((7,)), pltpu.SemaphoreType.DMA((7,))],
        compiler_params=pltpu.CompilerParams(
            collective_id=2, has_side_effects=True, vmem_limit_bytes=8 * 2**20
        ),
    )(dkv.reshape(HEADS, ROWS, LANES))
    shape = (ROWS, HEADS * HDIM)
    return pl.pallas_call(
        unpack_kernel,
        name="unpack",
        out_shape=(jax.ShapeDtypeStruct(shape, BF16),) * 3,
        in_specs=[VMEM_SPEC] * 2,
        out_specs=(HBM_SPEC,) * 3,
        scratch_shapes=[pltpu.VMEM(shape, BF16)] * 3 + [pltpu.SemaphoreType.DMA((3,))],
        compiler_params=pltpu.CompilerParams(vmem_limit_bytes=8 * 2**20),
    )(dq_got, dkv_got)


def body(queries, keys, values, out_grad, tile_mask, frame_order):
    kv, qg_mine, kv_own, qg_own, lists = enter(queries, keys, values, out_grad, tile_mask, frame_order)
    stats_own, dq = query_side(kv, qg_own, lists)
    qg, stats, dq_got = share(qg_mine, stats_own, dq)
    return leave(dq_got, key_side(qg, stats, kv_own, lists))


def solution(mesh):
    whole = P(("blk", "head"), None)
    return jax.shard_map(
        body,
        mesh=mesh,
        in_specs=(whole,) * 4 + (P(), P()),
        out_specs=(whole,) * 3,
        check_vma=False,
    )
```
